256 devices in a mesh: frames: 32 (over z, x_hi, core), heads: 8 (over y, x_lo).
Axes of the slice: x: 4 (x_hi: 2, x_lo: 2; x = x_hi * 2 + x_lo), y: 4, z: 8, core: 2. Of those that a mesh axis runs over, the one named last changes fastest.
Arguments:
- queries: bfloat16 [32768, 3072], P(('frames', 'heads')), may hold values from -6 to 6
- key_rows: bfloat16 [32768, 3072], P(('frames', 'heads')), may hold values from -6 to 6
- value_rows: bfloat16 [32768, 3072], P(('frames', 'heads')), may hold values from -6 to 6
- out_grad: bfloat16 [32768, 3072], P(('frames', 'heads')), may hold values from -6 to 6
- key_tiles: int32 [128, 8], P('frames'), may hold values from 0 to 127, as said below
- key_count: int32 [128], P('frames'), may hold values from 2 to 8, as said below
Outputs:
- attended: bfloat16 [32768, 3072], P(('frames', 'heads'))
- query_grad: bfloat16 [32768, 3072], P(('frames', 'heads'))
- key_grad: bfloat16 [32768, 3072], P(('frames', 'heads'))
- value_grad: bfloat16 [32768, 3072], P(('frames', 'heads'))
The draws below stay inside these ranges and needn't reach their ends.
Inputs may be any that keep to these rules, and one draw needn't show every extreme that they name: `key_tiles`: the first entry of each row is the row's own tile; a row may list the same tile id more than once; every id lies in the row's aligned group of 4 consecutive tiles or in one of the two neighbouring groups; entries at or after key_count are the row's own tile. `key_count`: some tile of every aligned group of 4 tiles uses all 8 entries.
All inputs are finite; a program needn't handle non-finite values.
Results may differ from the reference program's by a relative error of at most 0.022.
Values may be sent and summed in bfloat16 or wider, within the bound.
A program may use at most 128 MiB of HBM per device.

```python
import jax
import jax.numpy as jnp
from jax import lax

HEADS = 24
HEAD_DIM = 128
TILE = 256
KW = 8
TILES_DEV = 4
TILES = 128
TOKENS = 32768


def draw_queries(key, part):
    base = jax.random.normal(jax.random.fold_in(key, 11), (TOKENS, HEADS * HEAD_DIM), jnp.float32)
    return jnp.clip(base, -6.0, 6.0).astype(jnp.bfloat16)


def draw_key_rows(key, part):
    base = jax.random.normal(jax.random.fold_in(key, 12), (TOKENS, HEADS * HEAD_DIM), jnp.float32)
    return jnp.clip(base, -6.0, 6.0).astype(jnp.bfloat16)


def pattern_parts(key):
    tile_ids = jnp.arange(TILES, dtype=jnp.int32)
    group = tile_ids // TILES_DEV
    local = tile_ids % TILES_DEV
    last_group = TILES // TILES_DEV - 1
    prev_pick = jax.random.randint(jax.random.fold_in(key, 21), (TILES,), 0, TILES_DEV, jnp.int32)
    next_pick = jax.random.randint(jax.random.fold_in(key, 22), (TILES,), 0, TILES_DEV, jnp.int32)
    prev_base = (group - 1) * TILES_DEV
    next_base = (group + 1) * TILES_DEV
    own_base = group * TILES_DEV
    prev_a = prev_base + prev_pick
    prev_b = prev_base + (prev_pick + 1) % TILES_DEV
    next_a = next_base + next_pick
    next_b = next_base + (next_pick + 1) % TILES_DEV
    first_prev = jnp.where(group > 0, prev_a, next_base + (next_pick + 2) % TILES_DEV)
    second_prev = jnp.where(group > 0, prev_b, next_base + (next_pick + 3) % TILES_DEV)
    first_next = jnp.where(group < last_group, next_a, prev_base + (prev_pick + 2) % TILES_DEV)
    second_next = jnp.where(group < last_group, next_b, prev_base + (prev_pick + 3) % TILES_DEV)
    extra_prev = jnp.where(group > 0, first_prev, first_prev)
    own_one = own_base + (local + 1) % TILES_DEV
    own_two = own_base + (local + 2) % TILES_DEV
    own_three = own_base + (local + 3) % TILES_DEV
    fill_first = jnp.where(group > 0, jnp.where(group < last_group, next_a, prev_a), next_a)
    fill_second = jnp.where(group > 0, jnp.where(group < last_group, next_b, prev_b), next_b)
    entries = jnp.stack([tile_ids, extra_prev, first_next, own_one, second_prev, second_next, own_two, own_three], axis=1)
    entries = jnp.where((group == 0)[:, None] | (group == last_group)[:, None], jnp.stack([tile_ids, first_prev, fill_first, own_one, second_prev, fill_second, own_two, own_three], axis=1), entries)
    counts = jax.random.randint(jax.random.fold_in(key, 23), (TILES,), 2, KW + 1, jnp.int32)
    counts = jnp.where(local == 0, KW, counts).astype(jnp.int32)
    used = jnp.arange(KW, dtype=jnp.int32)[None, :] < counts[:, None]
    entries = jnp.where(used, entries, tile_ids[:, None]).astype(jnp.int32)
    return (entries, counts)


def draw_key_tiles(key, part):
    entries, counts = pattern_parts(key)
    return entries


def draw_key_count(key, part):
    entries, counts = pattern_parts(key)
    return counts


def block_scale(rng, shape, cuts, least, top_value):
    def one(dim, shards_of):
        draws = jax.random.uniform(jax.random.fold_in(jax.random.fold_in(rng, 6), dim), (shards_of,), jnp.float32, least / len(cuts), top_value / len(cuts))
        return jnp.repeat(jnp.exp(draws), shape[dim] // shards_of).reshape((-1,) + (1,) * (len(shape) - dim - 1))

    loudness = one(*cuts[0])
    for cut in cuts[1:]:
        loudness = loudness * one(*cut)
    return loudness


def centred(rng, extent, scale, most, split=(), kind=jnp.bfloat16):
    values = scale * jax.random.normal(rng, extent, jnp.float32)
    if split:
        values = values * block_scale(rng, extent, split, -0.22, 0.18)
    return jnp.clip(values, -most, most).astype(kind)


def setup_inputs(seed: int = 0) -> dict:
    key_of = jax.random.split(jax.random.key(seed), 7)
    queries = draw_queries(jax.random.fold_in(key_of[6], 71), 0)
    key_rows = draw_key_rows(jax.random.fold_in(key_of[6], 71), 0)
    value_rows = centred(key_of[2], (TOKENS, HEADS * HEAD_DIM), 1.0, 6.0, ((0, 256),))
    out_grad = centred(key_of[3], (TOKENS, HEADS * HEAD_DIM), 1.0, 6.0, ((0, 256),))
    key_tiles = draw_key_tiles(jax.random.fold_in(key_of[6], 71), 0)
    key_count = draw_key_count(jax.random.fold_in(key_of[6], 71), 0)
    return dict(queries=queries, key_rows=key_rows, value_rows=value_rows, out_grad=out_grad, key_tiles=key_tiles, key_count=key_count)


def reference(queries, key_rows, value_rows, out_grad, key_tiles, key_count):
    score_scale = HEAD_DIM ** -0.5
    features = HEADS * HEAD_DIM
    offsets = jnp.arange(TILE, dtype=jnp.int32)

    def per_tile(totals, inputs):
        tile_index, tile_ids, tile_count = inputs
        start = (tile_index * TILE).astype(jnp.int32)
        query_tile = lax.dynamic_slice_in_dim(queries, start, TILE, 0).astype(jnp.float32).reshape(TILE, HEADS, HEAD_DIM)
        grad_tile = lax.dynamic_slice_in_dim(out_grad, start, TILE, 0).astype(jnp.float32).reshape(TILE, HEADS, HEAD_DIM)
        key_index = (tile_ids[:, None] * TILE + offsets[None, :]).reshape(-1).astype(jnp.int32)
        key_sel = jnp.take(key_rows, key_index, axis=0).astype(jnp.float32).reshape(-1, HEADS, HEAD_DIM)
        value_sel = jnp.take(value_rows, key_index, axis=0).astype(jnp.float32).reshape(-1, HEADS, HEAD_DIM)
        allowed = jnp.repeat(jnp.arange(KW, dtype=jnp.int32) < tile_count, TILE)
        scores = jnp.einsum("qhd,khd->hqk", query_tile, key_sel) * score_scale
        scores = jnp.where(allowed[None, None, :], scores, -jnp.inf)
        highest = jnp.max(scores, axis=-1)
        log_total = highest + jnp.log(jnp.sum(jnp.exp(scores - highest[..., None]), axis=-1))
        weights = jnp.exp(scores - log_total[..., None])
        weights_low = lax.optimization_barrier(weights.astype(jnp.bfloat16)).astype(jnp.float32)
        attended = jnp.einsum("hqk,khd->qhd", weights_low, value_sel).astype(jnp.bfloat16)
        row_dots = jnp.einsum("qhd,qhd->hq", grad_tile, attended.astype(jnp.float32))
        d_weights = jnp.einsum("qhd,khd->hqk", grad_tile, value_sel)
        d_scores = weights * (d_weights - row_dots[..., None])
        d_scores = lax.optimization_barrier(d_scores.astype(jnp.bfloat16)).astype(jnp.float32)
        query_grad = (jnp.einsum("hqk,khd->qhd", d_scores, key_sel) * score_scale).astype(jnp.bfloat16)
        key_part = jnp.einsum("hqk,qhd->khd", d_scores, query_tile) * score_scale
        value_part = jnp.einsum("hqk,qhd->khd", weights_low, grad_tile)
        key_total = totals[0].at[key_index].add(key_part.reshape(-1, features))
        value_total = totals[1].at[key_index].add(value_part.reshape(-1, features))
        return (key_total, value_total), (attended.reshape(TILE, features), query_grad.reshape(TILE, features))

    zeros_grad = jnp.zeros((TOKENS, features), jnp.float32)
    tile_list = jnp.arange(TILES, dtype=jnp.int32)
    (key_total, value_total), (attended, query_grad) = lax.scan(per_tile, (zeros_grad, zeros_grad), (tile_list, key_tiles, key_count))
    return (attended.reshape(TOKENS, features), query_grad.reshape(TOKENS, features),
            key_total.astype(jnp.bfloat16), value_total.astype(jnp.bfloat16))
```

```python
import math

import jax
import jax.numpy as jnp
from jax import lax
from jax.experimental import pallas as pl
from jax.experimental.pallas import tpu as pltpu
from jax.sharding import PartitionSpec as P

HEAD_DIM = 128
TILE = 256
TILES_DEV = 4
ENTRIES = 8
NEAR = 3 * TILES_DEV
SLAB = TILES_DEV * TILE
SCALE = HEAD_DIM**-0.5
TO_LOG2 = SCALE * math.log2(math.e)
MASKED = -1e30
F32 = jnp.float32
BF16 = jnp.bfloat16
MESH = pl.DeviceIdType.MESH
ENTRY_ORDER = ((1, 0), (2, 0), (1, 1), (2, 1), (0, 0), (3, 0), (1, 2), (2, 2), (0, 1), (3, 1), (0, 2), (3, 2))
OFFSETS = ((0, 1), (1, 0), (3, 0), (2, 0), (1, 1), (3, 1), (2, 1))


def dot(a, b, a_dim, b_dim):
    return lax.dot_general(a, b, (((a_dim,), (b_dim,)), ((), ())), preferred_element_type=F32)


def tile_rows(tile):
    return pl.ds(pl.multiple_of(tile * TILE, TILE), TILE)


def flipped(index, flip):
    return index + flip * (1 - 2 * (index % 2))


def make_tables(base, key_tiles, key_count, slot_of, bias_of, entry_of):
    @pl.loop(0, TILES_DEV)
    def _(i):
        count = key_count[i]
        slots = [jnp.clip(key_tiles[i, e] - base, 0, NEAR - 1) for e in range(ENTRIES)]
        used = [(e < count).astype(jnp.int32) for e in range(ENTRIES)]
        firsts = []
        for e in range(ENTRIES):
            times = jnp.int32(0)
            before = jnp.int32(0)
            for other in range(ENTRIES):
                same = (slots[other] == slots[e]).astype(jnp.int32) * used[other]
                times = times + same
                if other < e:
                    before = before + same
            first = (before == 0).astype(jnp.int32) * used[e]
            bias = (1 - first).astype(F32) * MASKED
            for many in range(2, ENTRIES + 1):
                bias = bias + (first * (times == many).astype(jnp.int32)).astype(F32) * math.log2(many)
            firsts.append(first)
            slot_of[i, e] = slots[e]
            bias_of[i, e] = bias
        for j in range(NEAR):
            entry = jnp.int32(ENTRIES)
            for e in range(ENTRIES):
                entry = entry - (ENTRIES - e) * firsts[e] * (slots[e] == j).astype(jnp.int32)
            entry_of[i, j] = entry


def query_side(i, slot_of, bias_of, kw, vw, kt, vt, q, g, scores, weights, d_scores, g_low):
    best = jnp.full((8, TILE), -3e38, F32)
    for e in range(ENTRIES):
        s = dot(kw[slot_of[i, e]], q, 1, 1)
        scores[e] = s
        best = jnp.maximum(best, jnp.max(s.reshape(TILE // 8, 8, TILE), axis=0) + bias_of[i, e] * (1 / TO_LOG2))
    top = jnp.max(best, axis=0, keepdims=True) * TO_LOG2
    total = jnp.zeros((8, TILE), F32)
    out_t = jnp.zeros((HEAD_DIM, TILE), F32)
    for e in range(ENTRIES):
        p = jnp.exp2(scores[e] * TO_LOG2 - (top - bias_of[i, e]))
        total = total + jnp.sum(p.reshape(TILE // 8, 8, TILE), axis=0)
        p_low = p.astype(BF16)
        weights[i, e] = p_low
        out_t = out_t + dot(vt[slot_of[i, e]], p_low, 1, 0)
    inverse = 1.0 / jnp.sum(total, axis=0, keepdims=True)
    out_t = out_t * inverse
    g_t = (g.astype(F32).T * inverse).astype(BF16)
    g_low[i] = g_t
    row_dots = jnp.sum(g_t.astype(F32) * out_t, axis=0, keepdims=True)
    dq_t = jnp.zeros((HEAD_DIM, TILE), F32)
    for e in range(ENTRIES):
        dp = dot(vw[slot_of[i, e]], g_t, 1, 0)
        ds = (weights[i, e].astype(F32) * (dp - row_dots)).astype(BF16)
        d_scores[i, e] = ds
        dq_t = dq_t + dot(kt[slot_of[i, e]], ds, 1, 0)
    return out_t.T.astype(BF16), (dq_t * SCALE).T.astype(BF16)


def key_side(j, entry_of, q_of, weights, d_scores, g_low):
    dk = jnp.zeros((TILE, HEAD_DIM), F32)
    dv = jnp.zeros((TILE, HEAD_DIM), F32)
    for i in range(TILES_DEV):
        entry = entry_of[i, j]
        dk = dk + dot(d_scores[i, entry], q_of(i), 1, 0)
        dv = dv + dot(weights[i, entry], g_low[i], 1, 1)
    return dk * SCALE, dv


def kernel(
    frames, heads_dev, key_tiles, key_count, q_in, k_in, v_in, g_in, o_out, dq_out, dk_out, dv_out,
    slot_of, bias_of, entry_of, held, halo, grad_to, grad_from, leaving, kw, vw, kt, vt, scores, weights, d_scores, g_low,
    dk_own, dv_own, in_send, in_recv, halo_send, halo_recv, grad_send, grad_recv, out_send, out_recv,
):
    frame = lax.axis_index("frames")
    rank = lax.axis_index("heads")
    flip = (frame // 2) % 2
    row, side = rank // 2, rank % 2
    chunk = flipped(rank, flip)

    def partner(offset):
        return ((row + offset[0]) % 4) * 2 + (side + offset[1]) % 2

    neighbours = []
    for step in (frames - 1, 1):
        there = (frame + step) % frames
        neighbours.append({"frames": there, "heads": flipped(chunk, (there // 2) % 2)})

    barrier = pltpu.get_barrier_semaphore()
    for offset in OFFSETS:
        pl.semaphore_signal(barrier, inc=1, device_id={"frames": frame, "heads": partner(offset)}, device_id_type=MESH)
    for device in neighbours:
        pl.semaphore_signal(barrier, inc=1, device_id=device, device_id_type=MESH)
    pl.semaphore_wait(barrier, len(OFFSETS) + 2)

    def columns(of_chunk, h):
        return pl.ds(pl.multiple_of((of_chunk * heads_dev + h) * HEAD_DIM, HEAD_DIM), HEAD_DIM)

    def token_rows(of_rank):
        return pl.ds(pl.multiple_of(of_rank * 128, 128), 128)

    tensors = (q_in, k_in, v_in, g_in)
    outputs = (o_out, dq_out, dk_out, dv_out)

    for t, h in ENTRY_ORDER:
        for offset in OFFSETS:
            to = partner(offset)
            pltpu.make_async_remote_copy(
                src_ref=tensors[t].at[:, columns(flipped(to, flip), h)],
                dst_ref=held.at[t, h, token_rows(rank), :],
                send_sem=in_send.at[t, h],
                recv_sem=in_recv.at[t, h],
                device_id={"frames": frame, "heads": to},
                device_id_type=MESH,
            ).start()
        pltpu.make_async_copy(
            tensors[t].at[:, columns(chunk, h)], held.at[t, h, token_rows(rank), :], in_recv.at[t, h]
        ).start()

    def wait_bytes(ref, sem):
        pltpu.make_async_copy(ref, ref, sem).wait()

    def wait_in(t, h):
        wait_bytes(held.at[t, h], in_recv.at[t, h])

    def send_halo(h):
        for way in range(2):
            for kv in range(2):
                pltpu.make_async_remote_copy(
                    src_ref=held.at[1 + kv, h],
                    dst_ref=halo.at[h, 1 - way, kv],
                    send_sem=halo_send.at[h, way, kv],
                    recv_sem=halo_recv.at[h, 1 - way, kv],
                    device_id=neighbours[way],
                    device_id_type=MESH,
                ).start()

    def send_grads(h, way):
        for kv in range(2):
            pltpu.make_async_remote_copy(
                src_ref=grad_to.at[h, way, kv],
                dst_ref=grad_from.at[h, 1 - way, kv],
                send_sem=grad_send.at[h, way, kv],
                recv_sem=grad_recv.at[h, 1 - way, kv],
                device_id=neighbours[way],
                device_id_type=MESH,
            ).start()

    def send_out(t, h):
        for offset in OFFSETS:
            to = partner(offset)
            pltpu.make_async_remote_copy(
                src_ref=leaving.at[t, h, token_rows(to), :],
                dst_ref=outputs[t].at[:, columns(chunk, h)],
                send_sem=out_send.at[t, h],
                recv_sem=out_recv.at[t, h],
                device_id={"frames": frame, "heads": to},
                device_id_type=MESH,
            ).start()
        pltpu.make_async_copy(
            leaving.at[t, h, token_rows(rank), :], outputs[t].at[:, columns(chunk, h)], out_recv.at[t, h]
        ).start()

    make_tables((frame - 1) * TILES_DEV, key_tiles, key_count, slot_of, bias_of, entry_of)
    for i in range(TILES_DEV):
        weights[i, ENTRIES] = jnp.zeros((TILE, TILE), BF16)
        d_scores[i, ENTRIES] = jnp.zeros((TILE, TILE), BF16)

    for h in range(2):
        wait_in(1, h)
        wait_in(2, h)
        send_halo(h)

    def finish(h):
        for way in range(2):
            for kv in range(2):
                wait_bytes(grad_from.at[h, way, kv], grad_recv.at[h, way, kv])

        @pl.loop(0, TILES_DEV)
        def _(j):
            rows = tile_rows(j)
            for kv, own in ((0, dk_own), (1, dv_own)):
                whole = own[rows, :] + grad_from[h, 0, kv, rows, :].astype(F32) + grad_from[h, 1, kv, rows, :].astype(F32)
                leaving[2 + kv, h, rows, :] = whole.astype(BF16)

        send_out(2, h)
        send_out(3, h)

    @pl.loop(0, heads_dev)
    def _(h):
        wait_in(0, h)
        wait_in(3, h)
        for way in range(2):
            for kv in range(2):
                wait_bytes(halo.at[h, way, kv], halo_recv.at[h, way, kv])

        @pl.loop(0, TILES_DEV)
        def _(j):
            rows = tile_rows(j)
            for kv, flat, turned in ((0, kw, kt), (1, vw, vt)):
                for part, tile in enumerate((halo[h, 0, kv, rows, :], held[1 + kv, h, rows, :], halo[h, 1, kv, rows, :])):
                    flat[j + part * TILES_DEV] = tile
                    turned[j + part * TILES_DEV] = tile.T

        @pl.loop(0, TILES_DEV)
        def _(i):
            rows = tile_rows(i)
            out, dq = query_side(
                i, slot_of, bias_of, kw, vw, kt, vt, held[0, h, rows, :], held[3, h, rows, :], scores, weights, d_scores, g_low
            )
            leaving[0, h, rows, :] = out
            leaving[1, h, rows, :] = dq

        send_out(0, h)
        send_out(1, h)

        @pl.when(h == 0)
        def _():
            wait_in(1, 2)
            wait_in(2, 2)
            send_halo(2)

        @pl.when(h > 0)
        def _():
            finish(h - 1)

        def q_of(i):
            return held[0, h, i * TILE : (i + 1) * TILE, :]

        for way in (1, 0):
            @pl.loop(0, TILES_DEV)
            def _(j):
                dk, dv = key_side(j + way * 2 * TILES_DEV, entry_of, q_of, weights, d_scores, g_low)
                grad_to[h, way, 0, tile_rows(j), :] = dk.astype(BF16)
                grad_to[h, way, 1, tile_rows(j), :] = dv.astype(BF16)

            send_grads(h, way)

        @pl.loop(0, TILES_DEV)
        def _(j):
            dk, dv = key_side(j + TILES_DEV, entry_of, q_of, weights, d_scores, g_low)
            dk_own[tile_rows(j), :] = dk
            dv_own[tile_rows(j), :] = dv

    finish(heads_dev - 1)

    sent = SLAB - 128
    for h in range(heads_dev):
        for t in range(4):
            wait_bytes(held.at[t, h, 0:sent, :], in_send.at[t, h])
            wait_bytes(leaving.at[t, h, 0:sent, :], out_send.at[t, h])
            wait_bytes(leaving.at[t, h], out_recv.at[t, h])
        for way in range(2):
            for kv in range(2):
                wait_bytes(halo.at[h, way, kv], halo_send.at[h, way, kv])
                wait_bytes(grad_to.at[h, way, kv], grad_send.at[h, way, kv])


def on_device(queries, key_rows, value_rows, out_grad, key_tiles, key_count):
    frames = lax.axis_size("frames")
    tokens, features = queries.shape
    heads_dev = features // HEAD_DIM // lax.axis_size("heads")

    def body(*refs):
        kernel(frames, heads_dev, *refs)

    hbm = pl.BlockSpec(memory_space=pl.ANY)
    smem = pl.BlockSpec(memory_space=pltpu.SMEM)
    dma = pltpu.SemaphoreType.DMA
    return pl.pallas_call(
        body,
        out_shape=[jax.ShapeDtypeStruct((tokens, features), BF16)] * 4,
        in_specs=[smem, smem] + [hbm] * 4,
        out_specs=[hbm] * 4,
        scratch_shapes=[
            pltpu.SMEM((TILES_DEV, ENTRIES), jnp.int32),
            pltpu.SMEM((TILES_DEV, ENTRIES), F32),
            pltpu.SMEM((TILES_DEV, NEAR), jnp.int32),
            pltpu.VMEM((4, heads_dev, SLAB, HEAD_DIM), BF16),
            pltpu.VMEM((heads_dev, 2, 2, SLAB, HEAD_DIM), BF16),
            pltpu.VMEM((heads_dev, 2, 2, SLAB, HEAD_DIM), BF16),
            pltpu.VMEM((heads_dev, 2, 2, SLAB, HEAD_DIM), BF16),
            pltpu.VMEM((4, heads_dev, SLAB, HEAD_DIM), BF16),
            pltpu.VMEM((NEAR, TILE, HEAD_DIM), BF16),
            pltpu.VMEM((NEAR, TILE, HEAD_DIM), BF16),
            pltpu.VMEM((NEAR, HEAD_DIM, TILE), BF16),
            pltpu.VMEM((NEAR, HEAD_DIM, TILE), BF16),
            pltpu.VMEM((ENTRIES, TILE, TILE), F32),
            pltpu.VMEM((TILES_DEV, ENTRIES + 1, TILE, TILE), BF16),
            pltpu.VMEM((TILES_DEV, ENTRIES + 1, TILE, TILE), BF16),
            pltpu.VMEM((TILES_DEV, HEAD_DIM, TILE), BF16),
            pltpu.VMEM((SLAB, HEAD_DIM), F32),
            pltpu.VMEM((SLAB, HEAD_DIM), F32),
            dma((4, heads_dev)),
            dma((4, heads_dev)),
            dma((heads_dev, 2, 2)),
            dma((heads_dev, 2, 2)),
            dma((heads_dev, 2, 2)),
            dma((heads_dev, 2, 2)),
            dma((4, heads_dev)),
            dma((4, heads_dev)),
        ],
        compiler_params=pltpu.CompilerParams(collective_id=0, has_side_effects=True, vmem_limit_bytes=60 * 1024 * 1024),
        name="tile_attention",
    )(key_tiles, key_count, queries, key_rows, value_rows, out_grad)


def solution(mesh):
    spread = P(("frames", "heads"), None)
    return jax.shard_map(
        on_device,
        mesh=mesh,
        in_specs=(spread, spread, spread, spread, P("frames", None), P("frames")),
        out_specs=(spread, spread, spread, spread),
        check_vma=False,
    )
```

```python
import math

import jax
import jax.numpy as jnp
from jax import lax
from jax.experimental import pallas as pl
from jax.experimental.pallas import tpu as pltpu
from jax.sharding import PartitionSpec as P

HEAD_DIM = 128
TILE = 256
TILES_DEV = 4
ENTRIES = 8
NEAR = 3 * TILES_DEV
WIDE = 5 * TILES_DEV
SLAB = TILES_DEV * TILE
SCALE = HEAD_DIM**-0.5
TO_LOG2 = SCALE * math.log2(math.e)
MASKED = -1e30
F32 = jnp.float32
BF16 = jnp.bfloat16
MESH = pl.DeviceIdType.MESH
OFFSETS = ((0, 1), (1, 0), (3, 0), (2, 0), (1, 1), (3, 1), (2, 1))


def dot(a, b, a_dim, b_dim):
    return lax.dot_general(a, b, (((a_dim,), (b_dim,)), ((), ())), preferred_element_type=F32)


def tile_rows(tile):
    return pl.ds(pl.multiple_of(tile * TILE, TILE), TILE)


def flipped(index, flip):
    return index + flip * (1 - 2 * (index % 2))


def make_tables(first_row, base, tiles_at, count_at, slot_of, bias_of, entry_of):
    @pl.loop(0, TILES_DEV)
    def _(i):
        count = count_at(i)
        slots = [jnp.clip(tiles_at(i, e) - base, 0, NEAR - 1) for e in range(ENTRIES)]
        used = [(e < count).astype(jnp.int32) for e in range(ENTRIES)]
        firsts = []
        for e in range(ENTRIES):
            times = jnp.int32(0)
            before = jnp.int32(0)
            for other in range(ENTRIES):
                same = (slots[other] == slots[e]).astype(jnp.int32) * used[other]
                times = times + same
                if other < e:
                    before = before + same
            first = (before == 0).astype(jnp.int32) * used[e]
            bias = (1 - first).astype(F32) * MASKED
            for many in range(2, ENTRIES + 1):
                bias = bias + (first * (times == many).astype(jnp.int32)).astype(F32) * math.log2(many)
            firsts.append(first)
            slot_of[first_row + i, e] = slots[e]
            bias_of[first_row + i, e] = bias
        for j in range(NEAR):
            entry = jnp.int32(ENTRIES)
            for e in range(ENTRIES):
                entry = entry - (ENTRIES - e) * firsts[e] * (slots[e] == j).astype(jnp.int32)
            entry_of[first_row + i, j] = entry


def query_side(table, first_tile, at, slot_of, bias_of, kw, vw, kt, vt, q, g, scores, weights, d_scores, g_low):
    best = jnp.full((8, TILE), -3e38, F32)
    for e in range(ENTRIES):
        s = dot(kw[first_tile + slot_of[table, e]], q, 1, 1)
        scores[e] = s
        best = jnp.maximum(best, jnp.max(s.reshape(TILE // 8, 8, TILE), axis=0) + bias_of[table, e] * (1 / TO_LOG2))
    top = jnp.max(best, axis=0, keepdims=True) * TO_LOG2
    total = jnp.zeros((8, TILE), F32)
    out_t = jnp.zeros((HEAD_DIM, TILE), F32)
    for e in range(ENTRIES):
        p = jnp.exp2(scores[e] * TO_LOG2 - (top - bias_of[table, e]))
        total = total + jnp.sum(p.reshape(TILE // 8, 8, TILE), axis=0)
        p_low = p.astype(BF16)
        weights[at, e] = p_low
        out_t = out_t + dot(vt[first_tile + slot_of[table, e]], p_low, 1, 0)
    inverse = 1.0 / jnp.sum(total, axis=0, keepdims=True)
    out_t = out_t * inverse
    g_t = (g.astype(F32).T * inverse).astype(BF16)
    g_low[at] = g_t
    row_dots = jnp.sum(g_t.astype(F32) * out_t, axis=0, keepdims=True)
    dq_t = jnp.zeros((HEAD_DIM, TILE), F32)
    for e in range(ENTRIES):
        dp = dot(vw[first_tile + slot_of[table, e]], g_t, 1, 0)
        ds = (weights[at, e].astype(F32) * (dp - row_dots)).astype(BF16)
        d_scores[at, e] = ds
        dq_t = dq_t + dot(kt[first_tile + slot_of[table, e]], ds, 1, 0)
    return out_t.T.astype(BF16), (dq_t * SCALE).T.astype(BF16)


def key_side(parts, entry_of, q_of, weights, d_scores, g_low):
    dk = jnp.zeros((TILE, HEAD_DIM), F32)
    dv = jnp.zeros((TILE, HEAD_DIM), F32)
    for table, at, task, j in parts:
        for i in range(TILES_DEV):
            entry = entry_of[table + i, j]
            dk = dk + dot(d_scores[at + i, entry], q_of(task, i), 1, 0)
            dv = dv + dot(weights[at + i, entry], g_low[at + i], 1, 1)
    return dk * SCALE, dv


def kernel(
    frames, key_tiles, key_count, q_in, k_in, v_in, g_in, o_out, dq_out, dk_out, dv_out,
    far_table, slot_of, bias_of, entry_of, table_to, table_from, held, near_a, near_b, to_a, from_a, to_b, from_b, leaving,
    kw, vw, kt, vt, scores, weights, d_scores, g_low, dk_own, dv_own,
    in_send, in_recv, near_a_send, near_a_recv, near_b_send, near_b_recv, to_a_send, from_a_recv, to_b_send, from_b_recv,
    out_send, out_extra, out_recv, table_sems,
):
    frame = lax.axis_index("frames")
    rank = lax.axis_index("heads")
    core = frame % 2
    half = (frame // 2) % 2
    plane = (frame // 4) * 4
    row, side = rank // 2, rank % 2
    pair = flipped(rank, half)
    whole_head = pair * 3 + 2 * half
    split_head = pair * 3 + 1

    def device(of_frame, of_rank):
        return {"frames": of_frame, "heads": of_rank}

    def partner(offset):
        return ((row + offset[0]) % 4) * 2 + (side + offset[1]) % 2

    def member(of_half):
        return plane + 2 * of_half + core

    twin = device(frame + 1 - 2 * core, rank)
    above = device((frame + frames - 3 + 6 * core) % frames, rank)
    neighbours = []
    for step in (frames - 1, 1):
        there = (frame + step) % frames
        neighbours.append(device(there, flipped(pair, (there // 2) % 2)))
    table_peer = device(member(1 - half), flipped(rank, 1))

    barrier = pltpu.get_barrier_semaphore()
    greeted = [device(frame, partner(offset)) for offset in OFFSETS]
    greeted += [device(member(1 - half), partner(offset)) for offset in OFFSETS + ((0, 0),)]
    greeted += neighbours + [above]
    for peer in greeted:
        pl.semaphore_signal(barrier, inc=1, device_id=peer, device_id_type=MESH)

    table = jnp.zeros((8, 128), jnp.int32)
    at_row = lax.broadcasted_iota(jnp.int32, (8, 128), 0)
    at_lane = lax.broadcasted_iota(jnp.int32, (8, 128), 1)
    for i in range(TILES_DEV):
        for e in range(ENTRIES):
            table = jnp.where((at_row == i) & (at_lane == e), key_tiles[i, e], table)
        table = jnp.where((at_row == i) & (at_lane == ENTRIES), key_count[i], table)
    table_to[...] = table

    pl.semaphore_wait(barrier, len(greeted))

    def columns(head):
        return pl.ds(pl.multiple_of(head * HEAD_DIM, HEAD_DIM), HEAD_DIM)

    def token_rows(of_rank):
        return pl.ds(pl.multiple_of(of_rank * 128, 128), 128)

    def send(src, dst, send_sem, recv_sem, to):
        pltpu.make_async_remote_copy(
            src_ref=src, dst_ref=dst, send_sem=send_sem, recv_sem=recv_sem, device_id=to, device_id_type=MESH
        ).start()

    def wait_bytes(ref, sem):
        pltpu.make_async_copy(ref, ref, sem).wait()

    tensors = (q_in, k_in, v_in, g_in)
    outputs = (o_out, dq_out, dk_out, dv_out)

    def enter_whole(t):
        here = held.at[t, half, token_rows(rank), :]
        for turn in range(2):
            of_half = (half + turn) % 2
            for offset in OFFSETS + ((0, 0),) * turn:
                to = partner(offset)
                head = flipped(to, of_half) * 3 + 2 * of_half
                send(tensors[t].at[:, columns(head)], here, in_send.at[t, turn], in_recv.at[t, half], device(member(of_half), to))
        pltpu.make_async_copy(tensors[t].at[:, columns(whole_head)], here, in_recv.at[t, half]).start()

    def enter_split(t):
        here = held.at[t, 2, token_rows(rank), :]
        for offset in OFFSETS:
            to = partner(offset)
            send(tensors[t].at[:, columns(flipped(to, half) * 3 + 1)], here, in_send.at[t, 2], in_recv.at[t, 2], device(frame, to))
        pltpu.make_async_copy(tensors[t].at[:, columns(split_head)], here, in_recv.at[t, 2]).start()

    def leave_whole(t, task):
        there = outputs[t].at[:, columns(whole_head)]
        turn = (task + half) % 2
        for offset in OFFSETS:
            to = partner(offset)
            send(leaving.at[t, task, token_rows(to), :], there, out_send.at[t, task], out_recv.at[t, turn], device(member(task), to))

        @pl.when(turn == 0)
        def _():
            pltpu.make_async_copy(leaving.at[t, task, token_rows(rank), :], there, out_recv.at[t, 0]).start()

        @pl.when(turn == 1)
        def _():
            send(leaving.at[t, task, token_rows(rank), :], there, out_extra.at[t], out_recv.at[t, 1], device(member(1 - half), rank))

    def leave_split(t):
        there = outputs[t].at[:, columns(split_head)]
        for offset in OFFSETS:
            to = partner(offset)
            send(leaving.at[t, 2, token_rows(to), :], there, out_send.at[t, 2], out_recv.at[t, 2], device(frame, to))
        pltpu.make_async_copy(leaving.at[t, 2, token_rows(rank), :], there, out_recv.at[t, 2]).start()

    def wait_in(t, task):
        wait_bytes(held.at[t, task], in_recv.at[t, task])

    send(table_to, table_from, table_sems.at[0], table_sems.at[1], table_peer)
    for t in (1, 2, 0, 3):
        enter_whole(t)
    for t in (1, 2, 0, 3):
        enter_split(t)

    make_tables(
        half * TILES_DEV, (frame - 1) * TILES_DEV, lambda i, e: key_tiles[i, e], lambda i: key_count[i], slot_of, bias_of, entry_of
    )
    wait_bytes(table_from, table_sems.at[1])
    pltpu.make_async_copy(table_from, far_table, table_sems.at[2]).start()
    for i in range(2 * TILES_DEV):
        weights[i, ENTRIES] = jnp.zeros((TILE, TILE), BF16)
        d_scores[i, ENTRIES] = jnp.zeros((TILE, TILE), BF16)
    pltpu.make_async_copy(table_from, far_table, table_sems.at[2]).wait()
    make_tables(
        (1 - half) * TILES_DEV, (member(1 - half) - 1) * TILES_DEV,
        lambda i, e: far_table[i, e], lambda i: far_table[i, ENTRIES], slot_of, bias_of, entry_of,
    )

    for kv in range(2):
        for task in range(2):
            wait_in(1 + kv, task)
            send(
                held.at[1 + kv, task], near_a.at[task + core, kv], near_a_send.at[task, kv], near_a_recv.at[task, kv], twin
            )
        send(held.at[1 + kv, core], near_a.at[2 - 2 * core, kv], near_a_send.at[2, kv], near_a_recv.at[2, kv], above)

    def spread(tile, kv, block):
        (kw, vw)[kv][tile] = block
        (kt, vt)[kv][tile] = block.T

    @pl.loop(0, TILES_DEV)
    def _(j):
        for kv in range(2):
            for task in range(2):
                spread((2 * task + 1) * TILES_DEV + j, kv, held[1 + kv, task, tile_rows(j), :])

    def take_near(slot, sem):
        for kv in range(2):
            wait_bytes(near_a.at[slot, kv], near_a_recv.at[sem, kv])

        @pl.loop(0, TILES_DEV)
        def _(j):
            for kv in range(2):
                spread(2 * slot * TILES_DEV + j, kv, near_a[slot, kv, tile_rows(j), :])

    for task in range(2):
        take_near(task + 1 - core, task)

    def queries(task, table, first_tile, at):
        @pl.loop(0, TILES_DEV)
        def _(i):
            rows = tile_rows(i)
            out, dq = query_side(
                table + i, first_tile, at + i, slot_of, bias_of, kw, vw, kt, vt,
                held[0, task, rows, :], held[3, task, rows, :], scores, weights, d_scores, g_low,
            )
            leaving[0, task, rows, :] = out
            leaving[1, task, rows, :] = dq

    def q_of(task, i):
        return held[0, task, i * TILE : (i + 1) * TILE, :]

    def keys(put, *parts):
        @pl.loop(0, TILES_DEV)
        def _(j):
            dk, dv = key_side(
                [(table, at, task, j + part * TILES_DEV) for table, at, task, part in parts],
                entry_of, q_of, weights, d_scores, g_low,
            )
            put(tile_rows(j), dk, dv)

    def to_near(slot):
        def put(rows, dk, dv):
            to_a[slot, 0, rows, :] = dk.astype(BF16)
            to_a[slot, 1, rows, :] = dv.astype(BF16)

        return put

    def to_own(task):
        def put(rows, dk, dv):
            dk_own[task, rows, :] = dk
            dv_own[task, rows, :] = dv

        return put

    def whole_parts(task, part):
        return (task * TILES_DEV, task * TILES_DEV, task, part)

    def hand_over(slot, sem, at, to):
        for kv in range(2):
            send(to_a.at[slot, kv], from_a.at[at, kv], to_a_send.at[sem, kv], from_a_recv.at[at, kv], to)

    first, second = 1 - core, core
    wait_in(0, first)
    wait_in(3, first)
    queries(first, first * TILES_DEV, 2 * first * TILES_DEV, first * TILES_DEV)
    leave_whole(0, first)
    leave_whole(1, first)
    keys(to_near(2 * first), whole_parts(first, 2 * first))
    hand_over(2 * first, 0, first, twin)
    keys(to_own(first), whole_parts(first, 1))

    for kv in range(2):
        wait_in(1 + kv, 2)
        for way in range(2):
            send(
                held.at[1 + kv, 2], near_b.at[1 - way, kv], near_b_send.at[way, kv], near_b_recv.at[1 - way, kv], neighbours[way]
            )

    take_near(2 * core, 2)
    wait_in(0, second)
    wait_in(3, second)
    queries(second, second * TILES_DEV, 2 * second * TILES_DEV, second * TILES_DEV)
    leave_whole(0, second)
    leave_whole(1, second)
    keys(to_near(2 * second), whole_parts(second, 2 * second))
    hand_over(2 * second, 1, 2, above)
    keys(to_near(1), whole_parts(0, 2), whole_parts(1, 0))
    hand_over(1, 2, second, twin)
    keys(to_own(second), whole_parts(second, 1))

    wait_in(0, 2)
    wait_in(3, 2)
    for way in range(2):
        for kv in range(2):
            wait_bytes(near_b.at[way, kv], near_b_recv.at[way, kv])

    @pl.loop(0, TILES_DEV)
    def _(j):
        for kv in range(2):
            spread(j, kv, near_b[0, kv, tile_rows(j), :])
            spread(TILES_DEV + j, kv, held[1 + kv, 2, tile_rows(j), :])
            spread(2 * TILES_DEV + j, kv, near_b[1, kv, tile_rows(j), :])

    queries(2, half * TILES_DEV, 0, 0)
    leave_split(0)
    leave_split(1)

    for at in range(3):
        for kv in range(2):
            wait_bytes(from_a.at[at, kv], from_a_recv.at[at, kv])

    for task in range(2):
        border = (core == task).astype(F32)

        @pl.loop(0, TILES_DEV)
        def _(j):
            rows = tile_rows(j)
            for kv, own in ((0, dk_own), (1, dv_own)):
                total = own[task, rows, :] + from_a[task, kv, rows, :].astype(F32)
                total = total + border * from_a[2, kv, rows, :].astype(F32)
                leaving[2 + kv, task, rows, :] = total.astype(BF16)

        leave_whole(2, task)
        leave_whole(3, task)

    for way in (0, 1):
        def put(rows, dk, dv):
            to_b[way, 0, rows, :] = dk.astype(BF16)
            to_b[way, 1, rows, :] = dv.astype(BF16)

        keys(put, (half * TILES_DEV, 0, 2, 2 * way))
        for kv in range(2):
            send(to_b.at[way, kv], from_b.at[1 - way, kv], to_b_send.at[way, kv], from_b_recv.at[1 - way, kv], neighbours[way])
    keys(to_own(0), (half * TILES_DEV, 0, 2, 1))

    for kv, own in ((0, dk_own), (1, dv_own)):
        for way in range(2):
            wait_bytes(from_b.at[way, kv], from_b_recv.at[way, kv])

        @pl.loop(0, TILES_DEV)
        def _(j):
            rows = tile_rows(j)
            total = own[0, rows, :] + from_b[0, kv, rows, :].astype(F32) + from_b[1, kv, rows, :].astype(F32)
            leaving[2 + kv, 2, rows, :] = total.astype(BF16)

        leave_split(2 + kv)

    seven = SLAB - 128
    for t in range(4):
        wait_bytes(held.at[t, 0, 0:seven, :], in_send.at[t, 0])
        wait_bytes(held.at[t, 0], in_send.at[t, 1])
        wait_bytes(held.at[t, 0, 0:seven, :], in_send.at[t, 2])
        wait_bytes(leaving.at[t, 0, 0:128, :], out_extra.at[t])
        for task in range(3):
            wait_bytes(leaving.at[t, task, 0:seven, :], out_send.at[t, task])
            wait_bytes(leaving.at[t, task], out_recv.at[t, task])
    for kv in range(2):
        for at in range(3):
            wait_bytes(near_a.at[at, kv], near_a_send.at[at, kv])
            wait_bytes(to_a.at[at, kv], to_a_send.at[at, kv])
        for way in range(2):
            wait_bytes(near_b.at[way, kv], near_b_send.at[way, kv])
            wait_bytes(to_b.at[way, kv], to_b_send.at[way, kv])
    wait_bytes(table_to, table_sems.at[0])


def on_device(queries, key_rows, value_rows, out_grad, key_tiles, key_count):
    frames = lax.axis_size("frames")
    tokens, features = queries.shape

    def body(*refs):
        kernel(frames, *refs)

    hbm = pl.BlockSpec(memory_space=pl.ANY)
    smem = pl.BlockSpec(memory_space=pltpu.SMEM)
    dma = pltpu.SemaphoreType.DMA
    block = (SLAB, HEAD_DIM)
    return pl.pallas_call(
        body,
        out_shape=[jax.ShapeDtypeStruct((tokens, features), BF16)] * 4,
        in_specs=[smem, smem] + [hbm] * 4,
        out_specs=[hbm] * 4,
        scratch_shapes=[
            pltpu.SMEM((8, 128), jnp.int32),
            pltpu.SMEM((2 * TILES_DEV, ENTRIES), jnp.int32),
            pltpu.SMEM((2 * TILES_DEV, ENTRIES), F32),
            pltpu.SMEM((2 * TILES_DEV, NEAR), jnp.int32),
            pltpu.VMEM((8, 128), jnp.int32),
            pltpu.VMEM((8, 128), jnp.int32),
            pltpu.VMEM((4, 3) + block, BF16),
            pltpu.VMEM((3, 2) + block, BF16),
            pltpu.VMEM((2, 2) + block, BF16),
            pltpu.VMEM((3, 2) + block, BF16),
            pltpu.VMEM((3, 2) + block, BF16),
            pltpu.VMEM((2, 2) + block, BF16),
            pltpu.VMEM((2, 2) + block, BF16),
            pltpu.VMEM((4, 3) + block, BF16),
            pltpu.VMEM((WIDE, TILE, HEAD_DIM), BF16),
            pltpu.VMEM((WIDE, TILE, HEAD_DIM), BF16),
            pltpu.VMEM((WIDE, HEAD_DIM, TILE), BF16),
            pltpu.VMEM((WIDE, HEAD_DIM, TILE), BF16),
            pltpu.VMEM((ENTRIES, TILE, TILE), F32),
            pltpu.VMEM((2 * TILES_DEV, ENTRIES + 1, TILE, TILE), BF16),
            pltpu.VMEM((2 * TILES_DEV, ENTRIES + 1, TILE, TILE), BF16),
            pltpu.VMEM((2 * TILES_DEV, HEAD_DIM, TILE), BF16),
            pltpu.VMEM((2,) + block, F32),
            pltpu.VMEM((2,) + block, F32),
            dma((4, 3)),
            dma((4, 3)),
            dma((3, 2)),
            dma((3, 2)),
            dma((2, 2)),
            dma((2, 2)),
            dma((3, 2)),
            dma((3, 2)),
            dma((2, 2)),
            dma((2, 2)),
            dma((4, 3)),
            dma((4,)),
            dma((4, 3)),
            dma((3,)),
        ],
        compiler_params=pltpu.CompilerParams(collective_id=0, has_side_effects=True, vmem_limit_bytes=60 * 1024 * 1024),
        name="tile_attention",
    )(key_tiles, key_count, queries, key_rows, value_rows, out_grad)


def solution(mesh):
    spread = P(("frames", "heads"), None)
    return jax.shard_map(
        on_device,
        mesh=mesh,
        in_specs=(spread, spread, spread, spread, P("frames", None), P("frames")),
        out_specs=(spread, spread, spread, spread),
        check_vma=False,
    )
```

```python
import math

import jax
import jax.numpy as jnp
from jax import lax
from jax.experimental import pallas as pl
from jax.experimental.pallas import tpu as pltpu
from jax.sharding import PartitionSpec as P

HEAD_DIM = 128
TILE = 256
TILES_DEV = 4
ENTRIES = 8
NEAR = 3 * TILES_DEV
WIDE = 5 * TILES_DEV
SLAB = TILES_DEV * TILE
SCALE = HEAD_DIM**-0.5
TO_LOG2 = SCALE * math.log2(math.e)
MASKED = -1e30
PIECE = 32
F32 = jnp.float32
BF16 = jnp.bfloat16
MESH = pl.DeviceIdType.MESH
OFFSETS = ((0, 1), (1, 0), (3, 0), (2, 0), (1, 1), (3, 1), (2, 1))


def dot(a, b, a_dim, b_dim):
    return lax.dot_general(a, b, (((a_dim,), (b_dim,)), ((), ())), preferred_element_type=F32)


def tile_rows(tile):
    return pl.ds(pl.multiple_of(tile * TILE, TILE), TILE)


def flipped(index, flip):
    return index + flip * (1 - 2 * (index % 2))


def make_tables(first_row, base, tiles_at, count_at, slot_of, bias_of, entry_of):
    @pl.loop(0, TILES_DEV)
    def _(i):
        count = count_at(i)
        slots = [jnp.clip(tiles_at(i, e) - base, 0, NEAR - 1) for e in range(ENTRIES)]
        used = [(e < count).astype(jnp.int32) for e in range(ENTRIES)]
        firsts = []
        for e in range(ENTRIES):
            times = jnp.int32(0)
            before = jnp.int32(0)
            for other in range(ENTRIES):
                same = (slots[other] == slots[e]).astype(jnp.int32) * used[other]
                times = times + same
                if other < e:
                    before = before + same
            first = (before == 0).astype(jnp.int32) * used[e]
            bias = (1 - first).astype(F32) * MASKED
            for many in range(2, ENTRIES + 1):
                bias = bias + (first * (times == many).astype(jnp.int32)).astype(F32) * math.log2(many)
            firsts.append(first)
            slot_of[first_row + i, e] = slots[e]
            bias_of[first_row + i, e] = bias
        for j in range(NEAR):
            entry = jnp.int32(ENTRIES)
            for e in range(ENTRIES):
                entry = entry - (ENTRIES - e) * firsts[e] * (slots[e] == j).astype(jnp.int32)
            entry_of[first_row + i, j] = entry


def score(e, table, first_tile, slot_of, bias_of, kw, q, scores, best):
    s = dot(kw[first_tile + slot_of[table, e]], q, 1, 1)
    scores[e] = s
    return jnp.maximum(best, jnp.max(s.reshape(TILE // 8, 8, TILE), axis=0) + bias_of[table, e] * (1 / TO_LOG2))


def query_side(table, first_tile, at, slot_of, bias_of, vw, kt, vt, g, scores, weights, d_scores, g_low, best, score_next):
    top = jnp.max(best, axis=0, keepdims=True) * TO_LOG2
    total = jnp.zeros((8, TILE), F32)
    out_t = jnp.zeros((HEAD_DIM, TILE), F32)
    best_next = no_best()
    for e in range(ENTRIES):
        offset = top - bias_of[table, e]
        best_next = score_next(e, best_next)
        for part in range(TILE // PIECE):
            rows = slice(part * PIECE, (part + 1) * PIECE)
            p = jnp.exp2(scores[e, rows, :] * TO_LOG2 - offset)
            total = total + jnp.sum(p.reshape(PIECE // 8, 8, TILE), axis=0)
            weights[at, e, rows, :] = p.astype(BF16)
        out_t = out_t + dot(vt[first_tile + slot_of[table, e]], weights[at, e], 1, 0)
    inverse = 1.0 / jnp.sum(total, axis=0, keepdims=True)
    out_t = out_t * inverse
    g_t = (g.astype(F32).T * inverse).astype(BF16)
    g_low[at] = g_t
    row_dots = jnp.sum(g_t.astype(F32) * out_t, axis=0, keepdims=True)
    dq_t = jnp.zeros((HEAD_DIM, TILE), F32)
    for e in range(ENTRIES):
        dp = dot(vw[first_tile + slot_of[table, e]], g_t, 1, 0)
        ds = (weights[at, e].astype(F32) * (dp - row_dots)).astype(BF16)
        d_scores[at, e] = ds
        dq_t = dq_t + dot(kt[first_tile + slot_of[table, e]], ds, 1, 0)
    return out_t.T.astype(BF16), (dq_t * SCALE).T.astype(BF16), best_next


def no_best():
    return jnp.full((8, TILE), -3e38, F32)


def key_side(parts, entry_of, q_of, weights, d_scores, g_low):
    dk = jnp.zeros((TILE, HEAD_DIM), F32)
    dv = jnp.zeros((TILE, HEAD_DIM), F32)
    for table, at, task, j in parts:
        for i in range(TILES_DEV):
            dk = dk + dot(d_scores[at + i, entry_of[table + i, j]], q_of(task, i), 1, 0)
    for table, at, task, j in parts:
        for i in range(TILES_DEV):
            dv = dv + dot(weights[at + i, entry_of[table + i, j]], g_low[at + i], 1, 1)
    return dk * SCALE, dv


def kernel(
    frames, key_tiles, key_count, q_in, k_in, v_in, g_in, o_out, dq_out, dk_out, dv_out,
    far_table, slot_of, bias_of, entry_of, table_to, table_from, held, near_a, near_b, to_a, from_a, to_b, from_b, leaving,
    kw, vw, kt, vt, scores_even, scores_odd, weights, d_scores, g_low, dk_own, dv_own,
    in_send, in_recv, near_a_send, near_a_recv, near_b_send, near_b_recv, to_a_send, from_a_recv, to_b_send, from_b_recv,
    out_send, out_extra, out_recv, table_sems,
):
    frame = lax.axis_index("frames")
    rank = lax.axis_index("heads")
    core = frame % 2
    half = (frame // 2) % 2
    plane = (frame // 4) * 4
    row, side = rank // 2, rank % 2
    pair = flipped(rank, half)
    whole_head = pair * 3 + 2 * half
    split_head = pair * 3 + 1

    def device(of_frame, of_rank):
        return {"frames": of_frame, "heads": of_rank}

    def partner(offset):
        return ((row + offset[0]) % 4) * 2 + (side + offset[1]) % 2

    def member(of_half):
        return plane + 2 * of_half + core

    twin = device(frame + 1 - 2 * core, rank)
    above = device((frame + frames - 3 + 6 * core) % frames, rank)
    neighbours = []
    for step in (frames - 1, 1):
        there = (frame + step) % frames
        neighbours.append(device(there, flipped(pair, (there // 2) % 2)))
    table_peer = device(member(1 - half), flipped(rank, 1))

    barrier = pltpu.get_barrier_semaphore()
    greeted = [device(frame, partner(offset)) for offset in OFFSETS]
    greeted += [device(member(1 - half), partner(offset)) for offset in OFFSETS + ((0, 0),)]
    greeted += neighbours + [above]
    for peer in greeted:
        pl.semaphore_signal(barrier, inc=1, device_id=peer, device_id_type=MESH)

    table = jnp.zeros((8, 128), jnp.int32)
    at_row = lax.broadcasted_iota(jnp.int32, (8, 128), 0)
    at_lane = lax.broadcasted_iota(jnp.int32, (8, 128), 1)
    for i in range(TILES_DEV):
        for e in range(ENTRIES):
            table = jnp.where((at_row == i) & (at_lane == e), key_tiles[i, e], table)
        table = jnp.where((at_row == i) & (at_lane == ENTRIES), key_count[i], table)
    table_to[...] = table

    pl.semaphore_wait(barrier, len(greeted))

    def columns(head):
        return pl.ds(pl.multiple_of(head * HEAD_DIM, HEAD_DIM), HEAD_DIM)

    def token_rows(of_rank):
        return pl.ds(pl.multiple_of(of_rank * 128, 128), 128)

    def send(src, dst, send_sem, recv_sem, to):
        pltpu.make_async_remote_copy(
            src_ref=src, dst_ref=dst, send_sem=send_sem, recv_sem=recv_sem, device_id=to, device_id_type=MESH
        ).start()

    def wait_bytes(ref, sem):
        pltpu.make_async_copy(ref, ref, sem).wait()

    tensors = (q_in, k_in, v_in, g_in)
    outputs = (o_out, dq_out, dk_out, dv_out)

    def enter_whole(t):
        here = held.at[t, half, token_rows(rank), :]
        for turn in range(2):
            of_half = (half + turn) % 2
            for offset in OFFSETS + ((0, 0),) * turn:
                to = partner(offset)
                head = flipped(to, of_half) * 3 + 2 * of_half
                send(tensors[t].at[:, columns(head)], here, in_send.at[t, turn], in_recv.at[t, half], device(member(of_half), to))
        pltpu.make_async_copy(tensors[t].at[:, columns(whole_head)], here, in_recv.at[t, half]).start()

    def enter_split(t):
        here = held.at[t, 2, token_rows(rank), :]
        for offset in OFFSETS:
            to = partner(offset)
            send(tensors[t].at[:, columns(flipped(to, half) * 3 + 1)], here, in_send.at[t, 2], in_recv.at[t, 2], device(frame, to))
        pltpu.make_async_copy(tensors[t].at[:, columns(split_head)], here, in_recv.at[t, 2]).start()

    def leave_whole(t, task):
        there = outputs[t].at[:, columns(whole_head)]
        turn = (task + half) % 2
        for offset in OFFSETS:
            to = partner(offset)
            send(leaving.at[t, task, token_rows(to), :], there, out_send.at[t, task], out_recv.at[t, turn], device(member(task), to))

        @pl.when(turn == 0)
        def _():
            pltpu.make_async_copy(leaving.at[t, task, token_rows(rank), :], there, out_recv.at[t, 0]).start()

        @pl.when(turn == 1)
        def _():
            send(leaving.at[t, task, token_rows(rank), :], there, out_extra.at[t], out_recv.at[t, 1], device(member(1 - half), rank))

    def leave_split(t):
        there = outputs[t].at[:, columns(split_head)]
        for offset in OFFSETS:
            to = partner(offset)
            send(leaving.at[t, 2, token_rows(to), :], there, out_send.at[t, 2], out_recv.at[t, 2], device(frame, to))
        pltpu.make_async_copy(leaving.at[t, 2, token_rows(rank), :], there, out_recv.at[t, 2]).start()

    def wait_in(t, task):
        wait_bytes(held.at[t, task], in_recv.at[t, task])

    send(table_to, table_from, table_sems.at[0], table_sems.at[1], table_peer)
    first, second = 1 - core, core
    enter_whole(1)
    enter_whole(2)

    @pl.when(half == first)
    def _():
        enter_whole(0)
        enter_whole(3)

    enter_split(1)
    enter_split(2)

    @pl.when(half == second)
    def _():
        enter_whole(0)
        enter_whole(3)

    enter_split(0)
    enter_split(3)

    make_tables(
        half * TILES_DEV, (frame - 1) * TILES_DEV, lambda i, e: key_tiles[i, e], lambda i: key_count[i], slot_of, bias_of, entry_of
    )
    wait_bytes(table_from, table_sems.at[1])
    pltpu.make_async_copy(table_from, far_table, table_sems.at[2]).start()
    for i in range(2 * TILES_DEV):
        weights[i, ENTRIES] = jnp.zeros((TILE, TILE), BF16)
        d_scores[i, ENTRIES] = jnp.zeros((TILE, TILE), BF16)
    pltpu.make_async_copy(table_from, far_table, table_sems.at[2]).wait()
    make_tables(
        (1 - half) * TILES_DEV, (member(1 - half) - 1) * TILES_DEV,
        lambda i, e: far_table[i, e], lambda i: far_table[i, ENTRIES], slot_of, bias_of, entry_of,
    )

    for kv in range(2):
        for task in range(2):
            wait_in(1 + kv, task)
            send(
                held.at[1 + kv, task], near_a.at[task + core, kv], near_a_send.at[task, kv], near_a_recv.at[task, kv], twin
            )
        send(held.at[1 + kv, core], near_a.at[2 - 2 * core, kv], near_a_send.at[2, kv], near_a_recv.at[2, kv], above)

    def spread(tile, kv, block):
        (kw, vw)[kv][tile] = block
        (kt, vt)[kv][tile] = block.T

    @pl.loop(0, TILES_DEV)
    def _(j):
        for kv in range(2):
            for task in range(2):
                spread((2 * task + 1) * TILES_DEV + j, kv, held[1 + kv, task, tile_rows(j), :])

    def take_near(slot, sem):
        for kv in range(2):
            wait_bytes(near_a.at[slot, kv], near_a_recv.at[sem, kv])

        @pl.loop(0, TILES_DEV)
        def _(j):
            for kv in range(2):
                spread(2 * slot * TILES_DEV + j, kv, near_a[slot, kv, tile_rows(j), :])

    for task in range(2):
        take_near(task + 1 - core, task)

    def queries(task, table, first_tile, at):
        def score_of(i, scores):
            def one(e, best):
                return score(e, table + i, first_tile, slot_of, bias_of, kw, held[0, task, tile_rows(i), :], scores, best)

            return one

        def tile(i, scores, best, score_next):
            rows = tile_rows(i)
            out, dq, best = query_side(
                table + i, first_tile, at + i, slot_of, bias_of, vw, kt, vt, held[3, task, rows, :],
                scores, weights, d_scores, g_low, best, score_next,
            )
            leaving[0, task, rows, :] = out
            leaving[1, task, rows, :] = dq
            return best

        def two(k, best):
            best = tile(2 * k, scores_even, best, score_of(2 * k + 1, scores_odd))
            return tile(2 * k + 1, scores_odd, best, score_of((2 * k + 2) % TILES_DEV, scores_even))

        best = no_best()
        for e in range(ENTRIES):
            best = score_of(0, scores_even)(e, best)
        lax.fori_loop(0, TILES_DEV // 2, two, best)

    def q_of(task, i):
        return held[0, task, i * TILE : (i + 1) * TILE, :]

    def keys(put, *parts):
        @pl.loop(0, TILES_DEV, unroll=2)
        def _(j):
            dk, dv = key_side(
                [(table, at, task, j + part * TILES_DEV) for table, at, task, part in parts],
                entry_of, q_of, weights, d_scores, g_low,
            )
            put(tile_rows(j), dk, dv)

    def to_near(slot):
        def put(rows, dk, dv):
            to_a[slot, 0, rows, :] = dk.astype(BF16)
            to_a[slot, 1, rows, :] = dv.astype(BF16)

        return put

    def to_own(task):
        def put(rows, dk, dv):
            dk_own[task, rows, :] = dk
            dv_own[task, rows, :] = dv

        return put

    def whole_parts(task, part):
        return (task * TILES_DEV, task * TILES_DEV, task, part)

    def hand_over(slot, sem, at, to):
        for kv in range(2):
            send(to_a.at[slot, kv], from_a.at[at, kv], to_a_send.at[sem, kv], from_a_recv.at[at, kv], to)

    wait_in(0, first)
    wait_in(3, first)
    queries(first, first * TILES_DEV, 2 * first * TILES_DEV, first * TILES_DEV)
    leave_whole(0, first)
    leave_whole(1, first)
    keys(to_near(2 * first), whole_parts(first, 2 * first))
    hand_over(2 * first, 0, first, twin)
    keys(to_own(first), whole_parts(first, 1))

    for kv in range(2):
        wait_in(1 + kv, 2)
        for way in range(2):
            send(
                held.at[1 + kv, 2], near_b.at[1 - way, kv], near_b_send.at[way, kv], near_b_recv.at[1 - way, kv], neighbours[way]
            )

    take_near(2 * core, 2)
    wait_in(0, second)
    wait_in(3, second)
    queries(second, second * TILES_DEV, 2 * second * TILES_DEV, second * TILES_DEV)
    leave_whole(0, second)
    leave_whole(1, second)
    keys(to_near(2 * second), whole_parts(second, 2 * second))
    hand_over(2 * second, 1, 2, above)
    keys(to_near(1), whole_parts(0, 2), whole_parts(1, 0))
    hand_over(1, 2, second, twin)
    keys(to_own(second), whole_parts(second, 1))

    wait_in(0, 2)
    wait_in(3, 2)
    for way in range(2):
        for kv in range(2):
            wait_bytes(near_b.at[way, kv], near_b_recv.at[way, kv])

    @pl.loop(0, TILES_DEV)
    def _(j):
        for kv in range(2):
            spread(j, kv, near_b[0, kv, tile_rows(j), :])
            spread(TILES_DEV + j, kv, held[1 + kv, 2, tile_rows(j), :])
            spread(2 * TILES_DEV + j, kv, near_b[1, kv, tile_rows(j), :])

    queries(2, half * TILES_DEV, 0, 0)
    leave_split(0)
    leave_split(1)

    for at in range(3):
        for kv in range(2):
            wait_bytes(from_a.at[at, kv], from_a_recv.at[at, kv])

    for task in range(2):
        border = (core == task).astype(F32)

        @pl.loop(0, TILES_DEV)
        def _(j):
            rows = tile_rows(j)
            for kv, own in ((0, dk_own), (1, dv_own)):
                total = own[task, rows, :] + from_a[task, kv, rows, :].astype(F32)
                total = total + border * from_a[2, kv, rows, :].astype(F32)
                leaving[2 + kv, task, rows, :] = total.astype(BF16)

        leave_whole(2, task)
        leave_whole(3, task)

    for way in (0, 1):
        def put(rows, dk, dv):
            to_b[way, 0, rows, :] = dk.astype(BF16)
            to_b[way, 1, rows, :] = dv.astype(BF16)

        keys(put, (half * TILES_DEV, 0, 2, 2 * way))
        for kv in range(2):
            send(to_b.at[way, kv], from_b.at[1 - way, kv], to_b_send.at[way, kv], from_b_recv.at[1 - way, kv], neighbours[way])
    keys(to_own(0), (half * TILES_DEV, 0, 2, 1))

    for kv, own in ((0, dk_own), (1, dv_own)):
        for way in range(2):
            wait_bytes(from_b.at[way, kv], from_b_recv.at[way, kv])

        @pl.loop(0, TILES_DEV)
        def _(j):
            rows = tile_rows(j)
            total = own[0, rows, :] + from_b[0, kv, rows, :].astype(F32) + from_b[1, kv, rows, :].astype(F32)
            leaving[2 + kv, 2, rows, :] = total.astype(BF16)

        leave_split(2 + kv)

    seven = SLAB - 128
    for t in range(4):
        wait_bytes(held.at[t, 0, 0:seven, :], in_send.at[t, 0])
        wait_bytes(held.at[t, 0], in_send.at[t, 1])
        wait_bytes(held.at[t, 0, 0:seven, :], in_send.at[t, 2])
        wait_bytes(leaving.at[t, 0, 0:128, :], out_extra.at[t])
        for task in range(3):
            wait_bytes(leaving.at[t, task, 0:seven, :], out_send.at[t, task])
            wait_bytes(leaving.at[t, task], out_recv.at[t, task])
    for kv in range(2):
        for at in range(3):
            wait_bytes(near_a.at[at, kv], near_a_send.at[at, kv])
            wait_bytes(to_a.at[at, kv], to_a_send.at[at, kv])
        for way in range(2):
            wait_bytes(near_b.at[way, kv], near_b_send.at[way, kv])
            wait_bytes(to_b.at[way, kv], to_b_send.at[way, kv])
    wait_bytes(table_to, table_sems.at[0])


def copy_out(*refs):
    sources, results, pieces, sems = refs[:4], refs[4:8], refs[8], refs[9]
    inward = [pltpu.make_async_copy(sources[t], pieces.at[t], sems.at[0, t]) for t in range(4)]
    outward = [pltpu.make_async_copy(pieces.at[t], results[t], sems.at[1, t]) for t in range(4)]
    for copy in inward:
        copy.start()
    for t in range(4):
        inward[t].wait()
        outward[t].start()
    for copy in outward:
        copy.wait()


def on_device(queries, key_rows, value_rows, out_grad, key_tiles, key_count):
    frames = lax.axis_size("frames")
    tokens, features = queries.shape

    def body(*refs):
        kernel(frames, *refs)

    hbm = pl.BlockSpec(memory_space=pl.ANY)
    smem = pl.BlockSpec(memory_space=pltpu.SMEM)
    dma = pltpu.SemaphoreType.DMA
    block = (SLAB, HEAD_DIM)
    shapes = [jax.ShapeDtypeStruct((tokens, features), BF16)] * 4
    results = pl.pallas_call(
        body,
        out_shape=shapes,
        in_specs=[smem, smem] + [hbm] * 4,
        out_specs=[hbm] * 4,
        scratch_shapes=[
            pltpu.SMEM((8, 128), jnp.int32),
            pltpu.SMEM((2 * TILES_DEV, ENTRIES), jnp.int32),
            pltpu.SMEM((2 * TILES_DEV, ENTRIES), F32),
            pltpu.SMEM((2 * TILES_DEV, NEAR), jnp.int32),
            pltpu.VMEM((8, 128), jnp.int32),
            pltpu.VMEM((8, 128), jnp.int32),
            pltpu.VMEM((4, 3) + block, BF16),
            pltpu.VMEM((3, 2) + block, BF16),
            pltpu.VMEM((2, 2) + block, BF16),
            pltpu.VMEM((3, 2) + block, BF16),
            pltpu.VMEM((3, 2) + block, BF16),
            pltpu.VMEM((2, 2) + block, BF16),
            pltpu.VMEM((2, 2) + block, BF16),
            pltpu.VMEM((4, 3) + block, BF16),
            pltpu.VMEM((WIDE, TILE, HEAD_DIM), BF16),
            pltpu.VMEM((WIDE, TILE, HEAD_DIM), BF16),
            pltpu.VMEM((WIDE, HEAD_DIM, TILE), BF16),
            pltpu.VMEM((WIDE, HEAD_DIM, TILE), BF16),
            pltpu.VMEM((ENTRIES, TILE, TILE), F32),
            pltpu.VMEM((ENTRIES, TILE, TILE), F32),
            pltpu.VMEM((2 * TILES_DEV, ENTRIES + 1, TILE, TILE), BF16),
            pltpu.VMEM((2 * TILES_DEV, ENTRIES + 1, TILE, TILE), BF16),
            pltpu.VMEM((2 * TILES_DEV, HEAD_DIM, TILE), BF16),
            pltpu.VMEM((2,) + block, F32),
            pltpu.VMEM((2,) + block, F32),
            dma((4, 3)),
            dma((4, 3)),
            dma((3, 2)),
            dma((3, 2)),
            dma((2, 2)),
            dma((2, 2)),
            dma((3, 2)),
            dma((3, 2)),
            dma((2, 2)),
            dma((2, 2)),
            dma((4, 3)),
            dma((4,)),
            dma((4, 3)),
            dma((3,)),
        ],
        compiler_params=pltpu.CompilerParams(collective_id=0, has_side_effects=True, vmem_limit_bytes=60 * 1024 * 1024),
        name="tile_attention",
    )(key_tiles, key_count, queries, key_rows, value_rows, out_grad)
    return pl.pallas_call(
        copy_out,
        out_shape=shapes,
        in_specs=[hbm] * 4,
        out_specs=[hbm] * 4,
        scratch_shapes=[pltpu.VMEM((4, tokens, features), BF16), dma((2, 4))],
        name="copy_out",
    )(*results)


def solution(mesh):
    spread = P(("frames", "heads"), None)
    return jax.shard_map(
        on_device,
        mesh=mesh,
        in_specs=(spread, spread, spread, spread, P("frames", None), P("frames")),
        out_specs=(spread, spread, spread, spread),
        check_vma=False,
    )
```

```python
import math

import jax
import jax.numpy as jnp
from jax import lax
from jax.experimental import pallas as pl
from jax.experimental.pallas import tpu as pltpu
from jax.sharding import PartitionSpec as P

HEAD_DIM = 128
TILE = 256
TILES_DEV = 4
ENTRIES = 8
NEAR = 3 * TILES_DEV
WIDE = 5 * TILES_DEV
SLAB = TILES_DEV * TILE
SCALE = HEAD_DIM**-0.5
TO_LOG2 = SCALE * math.log2(math.e)
MASKED = -1e30
PIECE = 32
F32 = jnp.float32
BF16 = jnp.bfloat16
MESH = pl.DeviceIdType.MESH
OFFSETS = ((0, 1), (1, 0), (3, 0), (2, 0), (1, 1), (3, 1), (2, 1))


def dot(a, b, a_dim, b_dim):
    return lax.dot_general(a, b, (((a_dim,), (b_dim,)), ((), ())), preferred_element_type=F32)


def tile_rows(tile):
    return pl.ds(pl.multiple_of(tile * TILE, TILE), TILE)


def flipped(index, flip):
    return index + flip * (1 - 2 * (index % 2))


def make_tables(first_row, base, tiles_at, count_at, slot_of, bias_of, entry_of):
    @pl.loop(0, TILES_DEV)
    def _(i):
        count = count_at(i)
        slots = [jnp.clip(tiles_at(i, e) - base, 0, NEAR - 1) for e in range(ENTRIES)]
        used = [(e < count).astype(jnp.int32) for e in range(ENTRIES)]
        firsts = []
        for e in range(ENTRIES):
            times = jnp.int32(0)
            before = jnp.int32(0)
            for other in range(ENTRIES):
                same = (slots[other] == slots[e]).astype(jnp.int32) * used[other]
                times = times + same
                if other < e:
                    before = before + same
            first = (before == 0).astype(jnp.int32) * used[e]
            bias = (1 - first).astype(F32) * MASKED
            for many in range(2, ENTRIES + 1):
                bias = bias + (first * (times == many).astype(jnp.int32)).astype(F32) * math.log2(many)
            firsts.append(first)
            slot_of[first_row + i, e] = slots[e]
            bias_of[first_row + i, e] = bias
        for j in range(NEAR):
            entry = jnp.int32(ENTRIES)
            for e in range(ENTRIES):
                entry = entry - (ENTRIES - e) * firsts[e] * (slots[e] == j).astype(jnp.int32)
            entry_of[first_row + i, j] = entry


def score(e, table, first_tile, slot_of, bias_of, kw, q, scores, best):
    s = dot(kw[first_tile + slot_of[table, e]], q, 1, 1)
    scores[e] = s
    return jnp.maximum(best, jnp.max(s.reshape(TILE // 8, 8, TILE), axis=0) + bias_of[table, e] * (1 / TO_LOG2))


def query_side(table, first_tile, at, slot_of, bias_of, vw, kt, vt, g, scores, weights, d_scores, g_low, best, score_next):
    top = jnp.max(best, axis=0, keepdims=True) * TO_LOG2
    total = jnp.zeros((8, TILE), F32)
    out_t = jnp.zeros((HEAD_DIM, TILE), F32)
    best_next = no_best()
    for e in range(ENTRIES):
        offset = top - bias_of[table, e]
        best_next = score_next(e, best_next)
        for part in range(TILE // PIECE):
            rows = slice(part * PIECE, (part + 1) * PIECE)
            p = jnp.exp2(scores[e, rows, :] * TO_LOG2 - offset)
            total = total + jnp.sum(p.reshape(PIECE // 8, 8, TILE), axis=0)
            weights[at, e, rows, :] = p.astype(BF16)
        out_t = out_t + dot(vt[first_tile + slot_of[table, e]], weights[at, e], 1, 0)
    inverse = 1.0 / jnp.sum(total, axis=0, keepdims=True)
    out_t = out_t * inverse
    g_t = (g.astype(F32).T * inverse).astype(BF16)
    g_low[at] = g_t
    row_dots = jnp.sum(g_t.astype(F32) * out_t, axis=0, keepdims=True)
    dq_t = jnp.zeros((HEAD_DIM, TILE), F32)
    for e in range(ENTRIES):
        dp = dot(vw[first_tile + slot_of[table, e]], g_t, 1, 0)
        ds = (weights[at, e].astype(F32) * (dp - row_dots)).astype(BF16)
        d_scores[at, e] = ds
        dq_t = dq_t + dot(kt[first_tile + slot_of[table, e]], ds, 1, 0)
    return out_t.T.astype(BF16), (dq_t * SCALE).T.astype(BF16), best_next


def no_best():
    return jnp.full((8, TILE), -3e38, F32)


def key_side(parts, entry_of, q_of, weights, d_scores, g_low):
    dk = jnp.zeros((TILE, HEAD_DIM), F32)
    dv = jnp.zeros((TILE, HEAD_DIM), F32)
    for table, at, task, j in parts:
        for i in range(TILES_DEV):
            dk = dk + dot(d_scores[at + i, entry_of[table + i, j]], q_of(task, i), 1, 0)
    for table, at, task, j in parts:
        for i in range(TILES_DEV):
            dv = dv + dot(weights[at + i, entry_of[table + i, j]], g_low[at + i], 1, 1)
    return dk * SCALE, dv


def kernel(
    frames, key_tiles, key_count, q_in, k_in, v_in, g_in, o_out, dq_out, dk_out, dv_out,
    far_table, slot_of, bias_of, entry_of, table_to, table_from, held, near_a, near_b, to_a, from_a, to_b, from_b, leaving,
    kw, vw, kt, vt, scores_even, scores_odd, weights, d_scores, g_low, dk_own, dv_own,
    in_send, in_recv, near_a_send, near_a_recv, near_b_send, near_b_recv, to_a_send, from_a_recv, to_b_send, from_b_recv,
    out_send, out_extra, out_recv, table_sems,
):
    frame = lax.axis_index("frames")
    rank = lax.axis_index("heads")
    core = frame % 2
    half = (frame // 2) % 2
    plane = (frame // 4) * 4
    row, side = rank // 2, rank % 2
    pair = flipped(rank, half)
    whole_head = pair * 3 + 2 * half
    split_head = pair * 3 + 1

    def device(of_frame, of_rank):
        return {"frames": of_frame, "heads": of_rank}

    def partner(offset):
        return ((row + offset[0]) % 4) * 2 + (side + offset[1]) % 2

    def member(of_half):
        return plane + 2 * of_half + core

    twin = device(frame + 1 - 2 * core, rank)
    above = device((frame + frames - 3 + 6 * core) % frames, rank)
    neighbours = []
    for step in (frames - 1, 1):
        there = (frame + step) % frames
        neighbours.append(device(there, flipped(pair, (there // 2) % 2)))
    table_peer = device(member(1 - half), flipped(rank, 1))

    barrier = pltpu.get_barrier_semaphore()
    greeted = [device(frame, partner(offset)) for offset in OFFSETS]
    greeted += [device(member(1 - half), partner(offset)) for offset in OFFSETS + ((0, 0),)]
    greeted += neighbours + [above]
    for peer in greeted:
        pl.semaphore_signal(barrier, inc=1, device_id=peer, device_id_type=MESH)

    table = jnp.zeros((8, 128), jnp.int32)
    at_row = lax.broadcasted_iota(jnp.int32, (8, 128), 0)
    at_lane = lax.broadcasted_iota(jnp.int32, (8, 128), 1)
    for i in range(TILES_DEV):
        for e in range(ENTRIES):
            table = jnp.where((at_row == i) & (at_lane == e), key_tiles[i, e], table)
        table = jnp.where((at_row == i) & (at_lane == ENTRIES), key_count[i], table)
    table_to[...] = table

    pl.semaphore_wait(barrier, len(greeted))

    def columns(head):
        return pl.ds(pl.multiple_of(head * HEAD_DIM, HEAD_DIM), HEAD_DIM)

    def token_rows(of_rank):
        return pl.ds(pl.multiple_of(of_rank * 128, 128), 128)

    def send(src, dst, send_sem, recv_sem, to):
        pltpu.make_async_remote_copy(
            src_ref=src, dst_ref=dst, send_sem=send_sem, recv_sem=recv_sem, device_id=to, device_id_type=MESH
        ).start()

    def wait_bytes(ref, sem):
        pltpu.make_async_copy(ref, ref, sem).wait()

    tensors = (q_in, k_in, v_in, g_in)
    outputs = (o_out, dq_out, dk_out, dv_out)

    def enter_whole(t):
        here = held.at[t, half, token_rows(rank), :]
        for turn in range(2):
            of_half = (half + turn) % 2
            for offset in OFFSETS + ((0, 0),) * turn:
                to = partner(offset)
                head = flipped(to, of_half) * 3 + 2 * of_half
                send(tensors[t].at[:, columns(head)], here, in_send.at[t, turn], in_recv.at[t, half], device(member(of_half), to))
        pltpu.make_async_copy(tensors[t].at[:, columns(whole_head)], here, in_recv.at[t, half]).start()

    def enter_split(t):
        here = held.at[t, 2, token_rows(rank), :]
        for offset in OFFSETS:
            to = partner(offset)
            send(tensors[t].at[:, columns(flipped(to, half) * 3 + 1)], here, in_send.at[t, 2], in_recv.at[t, 2], device(frame, to))
        pltpu.make_async_copy(tensors[t].at[:, columns(split_head)], here, in_recv.at[t, 2]).start()

    def leave_whole(t, task):
        there = outputs[t].at[:, columns(whole_head)]
        turn = (task + half) % 2
        for offset in OFFSETS:
            to = partner(offset)
            send(leaving.at[t, task, token_rows(to), :], there, out_send.at[t, task], out_recv.at[t, turn], device(member(task), to))

        @pl.when(turn == 0)
        def _():
            pltpu.make_async_copy(leaving.at[t, task, token_rows(rank), :], there, out_recv.at[t, 0]).start()

        @pl.when(turn == 1)
        def _():
            send(leaving.at[t, task, token_rows(rank), :], there, out_extra.at[t], out_recv.at[t, 1], device(member(1 - half), rank))

    def leave_split(t):
        there = outputs[t].at[:, columns(split_head)]
        for offset in OFFSETS:
            to = partner(offset)
            send(leaving.at[t, 2, token_rows(to), :], there, out_send.at[t, 2], out_recv.at[t, 2], device(frame, to))
        pltpu.make_async_copy(leaving.at[t, 2, token_rows(rank), :], there, out_recv.at[t, 2]).start()

    def wait_in(t, task):
        wait_bytes(held.at[t, task], in_recv.at[t, task])

    send(table_to, table_from, table_sems.at[0], table_sems.at[1], table_peer)
    first, second = 1 - core, core
    enter_whole(1)
    enter_whole(2)

    @pl.when(half == first)
    def _():
        enter_whole(0)
        enter_whole(3)


    make_tables(
        half * TILES_DEV, (frame - 1) * TILES_DEV, lambda i, e: key_tiles[i, e], lambda i: key_count[i], slot_of, bias_of, entry_of
    )
    wait_bytes(table_from, table_sems.at[1])
    pltpu.make_async_copy(table_from, far_table, table_sems.at[2]).start()
    for i in range(2 * TILES_DEV):
        weights[i, ENTRIES] = jnp.zeros((TILE, TILE), BF16)
        d_scores[i, ENTRIES] = jnp.zeros((TILE, TILE), BF16)
    pltpu.make_async_copy(table_from, far_table, table_sems.at[2]).wait()
    make_tables(
        (1 - half) * TILES_DEV, (member(1 - half) - 1) * TILES_DEV,
        lambda i, e: far_table[i, e], lambda i: far_table[i, ENTRIES], slot_of, bias_of, entry_of,
    )

    for kv in range(2):
        for task in range(2):
            wait_in(1 + kv, task)
            send(
                held.at[1 + kv, task], near_a.at[task + core, kv], near_a_send.at[task, kv], near_a_recv.at[task, kv], twin
            )
        send(held.at[1 + kv, core], near_a.at[2 - 2 * core, kv], near_a_send.at[2, kv], near_a_recv.at[2, kv], above)

    def spread(tile, kv, block):
        (kw, vw)[kv][tile] = block
        (kt, vt)[kv][tile] = block.T

    @pl.loop(0, TILES_DEV)
    def _(j):
        for kv in range(2):
            for task in range(2):
                spread((2 * task + 1) * TILES_DEV + j, kv, held[1 + kv, task, tile_rows(j), :])

    def take_near(slot, sem):
        for kv in range(2):
            wait_bytes(near_a.at[slot, kv], near_a_recv.at[sem, kv])

        @pl.loop(0, TILES_DEV)
        def _(j):
            for kv in range(2):
                spread(2 * slot * TILES_DEV + j, kv, near_a[slot, kv, tile_rows(j), :])

    for task in range(2):
        take_near(task + 1 - core, task)

    def queries(task, table, first_tile, at, between=None):
        def score_of(i, scores):
            def one(e, best):
                return score(e, table + i, first_tile, slot_of, bias_of, kw, held[0, task, tile_rows(i), :], scores, best)

            return one

        def tile(i, scores, best, score_next):
            rows = tile_rows(i)
            out, dq, best = query_side(
                table + i, first_tile, at + i, slot_of, bias_of, vw, kt, vt, held[3, task, rows, :],
                scores, weights, d_scores, g_low, best, score_next,
            )
            leaving[0, task, rows, :] = out
            leaving[1, task, rows, :] = dq
            return best

        def two(k, best):
            best = tile(2 * k, scores_even, best, score_of(2 * k + 1, scores_odd))
            return tile(2 * k + 1, scores_odd, best, score_of((2 * k + 2) % TILES_DEV, scores_even))

        best = no_best()
        for e in range(ENTRIES):
            best = score_of(0, scores_even)(e, best)
        if between is None:
            lax.fori_loop(0, TILES_DEV // 2, two, best)
        else:
            best = two(0, best)
            between()
            two(1, best)

    def q_of(task, i):
        return held[0, task, i * TILE : (i + 1) * TILE, :]

    def keys(put, *parts):
        @pl.loop(0, TILES_DEV, unroll=2)
        def _(j):
            dk, dv = key_side(
                [(table, at, task, j + part * TILES_DEV) for table, at, task, part in parts],
                entry_of, q_of, weights, d_scores, g_low,
            )
            put(tile_rows(j), dk, dv)

    def to_near(slot):
        def put(rows, dk, dv):
            to_a[slot, 0, rows, :] = dk.astype(BF16)
            to_a[slot, 1, rows, :] = dv.astype(BF16)

        return put

    def to_own(task):
        def put(rows, dk, dv):
            dk_own[task, rows, :] = dk
            dv_own[task, rows, :] = dv

        return put

    def whole_parts(task, part):
        return (task * TILES_DEV, task * TILES_DEV, task, part)

    def hand_over(slot, sem, at, to):
        for kv in range(2):
            send(to_a.at[slot, kv], from_a.at[at, kv], to_a_send.at[sem, kv], from_a_recv.at[at, kv], to)

    wait_in(0, first)
    wait_in(3, first)
    enter_split(1)
    enter_split(2)

    @pl.when(half == second)
    def _():
        enter_whole(0)
        enter_whole(3)

    queries(first, first * TILES_DEV, 2 * first * TILES_DEV, first * TILES_DEV)
    for kv in range(2):
        wait_in(1 + kv, 2)
        for way in range(2):
            send(
                held.at[1 + kv, 2], near_b.at[1 - way, kv], near_b_send.at[way, kv], near_b_recv.at[1 - way, kv], neighbours[way]
            )

    enter_split(0)
    enter_split(3)
    leave_whole(0, first)
    leave_whole(1, first)
    keys(to_near(2 * first), whole_parts(first, 2 * first))
    hand_over(2 * first, 0, first, twin)
    keys(to_own(first), whole_parts(first, 1))

    take_near(2 * core, 2)
    wait_in(0, second)
    wait_in(3, second)
    queries(second, second * TILES_DEV, 2 * second * TILES_DEV, second * TILES_DEV)
    leave_whole(0, second)
    leave_whole(1, second)
    keys(to_near(2 * second), whole_parts(second, 2 * second))
    hand_over(2 * second, 1, 2, above)
    keys(to_near(1), whole_parts(0, 2), whole_parts(1, 0))
    hand_over(1, 2, second, twin)
    keys(to_own(second), whole_parts(second, 1))

    wait_in(0, 2)
    wait_in(3, 2)
    for way in range(2):
        for kv in range(2):
            wait_bytes(near_b.at[way, kv], near_b_recv.at[way, kv])

    @pl.loop(0, TILES_DEV)
    def _(j):
        for kv in range(2):
            spread(j, kv, near_b[0, kv, tile_rows(j), :])
            spread(TILES_DEV + j, kv, held[1 + kv, 2, tile_rows(j), :])
            spread(2 * TILES_DEV + j, kv, near_b[1, kv, tile_rows(j), :])

    def finish_whole():
        for at in range(3):
            for kv in range(2):
                wait_bytes(from_a.at[at, kv], from_a_recv.at[at, kv])

        for task in range(2):
            border = (core == task).astype(F32)

            @pl.loop(0, TILES_DEV)
            def _(j):
                rows = tile_rows(j)
                for kv, own in ((0, dk_own), (1, dv_own)):
                    total = own[task, rows, :] + from_a[task, kv, rows, :].astype(F32)
                    total = total + border * from_a[2, kv, rows, :].astype(F32)
                    leaving[2 + kv, task, rows, :] = total.astype(BF16)

            leave_whole(2, task)
            leave_whole(3, task)

    queries(2, half * TILES_DEV, 0, 0, finish_whole)
    for way in (0, 1):
        def put(rows, dk, dv):
            to_b[way, 0, rows, :] = dk.astype(BF16)
            to_b[way, 1, rows, :] = dv.astype(BF16)

        keys(put, (half * TILES_DEV, 0, 2, 2 * way))
        for kv in range(2):
            send(to_b.at[way, kv], from_b.at[1 - way, kv], to_b_send.at[way, kv], from_b_recv.at[1 - way, kv], neighbours[way])
    leave_split(0)
    leave_split(1)

    keys(to_own(0), (half * TILES_DEV, 0, 2, 1))

    for kv, own in ((0, dk_own), (1, dv_own)):
        for way in range(2):
            wait_bytes(from_b.at[way, kv], from_b_recv.at[way, kv])

        @pl.loop(0, TILES_DEV)
        def _(j):
            rows = tile_rows(j)
            total = own[0, rows, :] + from_b[0, kv, rows, :].astype(F32) + from_b[1, kv, rows, :].astype(F32)
            leaving[2 + kv, 2, rows, :] = total.astype(BF16)

        leave_split(2 + kv)

    seven = SLAB - 128
    for t in range(4):
        wait_bytes(held.at[t, 0, 0:seven, :], in_send.at[t, 0])
        wait_bytes(held.at[t, 0], in_send.at[t, 1])
        wait_bytes(held.at[t, 0, 0:seven, :], in_send.at[t, 2])
        wait_bytes(leaving.at[t, 0, 0:128, :], out_extra.at[t])
        for task in range(3):
            wait_bytes(leaving.at[t, task, 0:seven, :], out_send.at[t, task])
            wait_bytes(leaving.at[t, task], out_recv.at[t, task])
    for kv in range(2):
        for at in range(3):
            wait_bytes(near_a.at[at, kv], near_a_send.at[at, kv])
            wait_bytes(to_a.at[at, kv], to_a_send.at[at, kv])
        for way in range(2):
            wait_bytes(near_b.at[way, kv], near_b_send.at[way, kv])
            wait_bytes(to_b.at[way, kv], to_b_send.at[way, kv])
    wait_bytes(table_to, table_sems.at[0])


def copy_out(*refs):
    sources, results, pieces, sems = refs[:4], refs[4:8], refs[8], refs[9]
    inward = [pltpu.make_async_copy(sources[t], pieces.at[t], sems.at[0, t]) for t in range(4)]
    outward = [pltpu.make_async_copy(pieces.at[t], results[t], sems.at[1, t]) for t in range(4)]
    for copy in inward:
        copy.start()
    for t in range(4):
        inward[t].wait()
        outward[t].start()
    for copy in outward:
        copy.wait()


def on_device(queries, key_rows, value_rows, out_grad, key_tiles, key_count):
    frames = lax.axis_size("frames")
    tokens, features = queries.shape

    def body(*refs):
        kernel(frames, *refs)

    hbm = pl.BlockSpec(memory_space=pl.ANY)
    smem = pl.BlockSpec(memory_space=pltpu.SMEM)
    dma = pltpu.SemaphoreType.DMA
    block = (SLAB, HEAD_DIM)
    shapes = [jax.ShapeDtypeStruct((tokens, features), BF16)] * 4
    results = pl.pallas_call(
        body,
        out_shape=shapes,
        in_specs=[smem, smem] + [hbm] * 4,
        out_specs=[hbm] * 4,
        scratch_shapes=[
            pltpu.SMEM((8, 128), jnp.int32),
            pltpu.SMEM((2 * TILES_DEV, ENTRIES), jnp.int32),
            pltpu.SMEM((2 * TILES_DEV, ENTRIES), F32),
            pltpu.SMEM((2 * TILES_DEV, NEAR), jnp.int32),
            pltpu.VMEM((8, 128), jnp.int32),
            pltpu.VMEM((8, 128), jnp.int32),
            pltpu.VMEM((4, 3) + block, BF16),
            pltpu.VMEM((3, 2) + block, BF16),
            pltpu.VMEM((2, 2) + block, BF16),
            pltpu.VMEM((3, 2) + block, BF16),
            pltpu.VMEM((3, 2) + block, BF16),
            pltpu.VMEM((2, 2) + block, BF16),
            pltpu.VMEM((2, 2) + block, BF16),
            pltpu.VMEM((4, 3) + block, BF16),
            pltpu.VMEM((WIDE, TILE, HEAD_DIM), BF16),
            pltpu.VMEM((WIDE, TILE, HEAD_DIM), BF16),
            pltpu.VMEM((WIDE, HEAD_DIM, TILE), BF16),
            pltpu.VMEM((WIDE, HEAD_DIM, TILE), BF16),
            pltpu.VMEM((ENTRIES, TILE, TILE), F32),
            pltpu.VMEM((ENTRIES, TILE, TILE), F32),
            pltpu.VMEM((2 * TILES_DEV, ENTRIES + 1, TILE, TILE), BF16),
            pltpu.VMEM((2 * TILES_DEV, ENTRIES + 1, TILE, TILE), BF16),
            pltpu.VMEM((2 * TILES_DEV, HEAD_DIM, TILE), BF16),
            pltpu.VMEM((2,) + block, F32),
            pltpu.VMEM((2,) + block, F32),
            dma((4, 3)),
            dma((4, 3)),
            dma((3, 2)),
            dma((3, 2)),
            dma((2, 2)),
            dma((2, 2)),
            dma((3, 2)),
            dma((3, 2)),
            dma((2, 2)),
            dma((2, 2)),
            dma((4, 3)),
            dma((4,)),
            dma((4, 3)),
            dma((3,)),
        ],
        compiler_params=pltpu.CompilerParams(collective_id=0, has_side_effects=True, vmem_limit_bytes=60 * 1024 * 1024),
        name="tile_attention",
    )(key_tiles, key_count, queries, key_rows, value_rows, out_grad)
    return pl.pallas_call(
        copy_out,
        out_shape=shapes,
        in_specs=[hbm] * 4,
        out_specs=[hbm] * 4,
        scratch_shapes=[pltpu.VMEM((4, tokens, features), BF16), dma((2, 4))],
        name="copy_out",
    )(*results)


def solution(mesh):
    spread = P(("frames", "heads"), None)
    return jax.shard_map(
        on_device,
        mesh=mesh,
        in_specs=(spread, spread, spread, spread, P("frames", None), P("frames")),
        out_specs=(spread, spread, spread, spread),
        check_vma=False,
    )
```

```python
import math

import jax
import jax.numpy as jnp
from jax import lax
from jax.experimental import pallas as pl
from jax.experimental.pallas import tpu as pltpu
from jax.sharding import PartitionSpec as P

HEAD_DIM = 128
TILE = 256
TILES_DEV = 4
ENTRIES = 8
NEAR = 3 * TILES_DEV
WIDE = 5 * TILES_DEV
SLAB = TILES_DEV * TILE
SCALE = HEAD_DIM**-0.5
TO_LOG2 = SCALE * math.log2(math.e)
MASKED = -1e30
PIECE = 32
F32 = jnp.float32
BF16 = jnp.bfloat16
MESH = pl.DeviceIdType.MESH
OFFSETS = ((0, 1), (1, 0), (3, 0), (2, 0), (1, 1), (3, 1), (2, 1))


def dot(a, b, a_dim, b_dim):
    return lax.dot_general(a, b, (((a_dim,), (b_dim,)), ((), ())), preferred_element_type=F32)


def tile_rows(tile):
    return pl.ds(pl.multiple_of(tile * TILE, TILE), TILE)


def flipped(index, flip):
    return index + flip * (1 - 2 * (index % 2))


def make_tables(first_row, base, tiles_at, count_at, slot_of, bias_of, entry_of):
    @pl.loop(0, TILES_DEV)
    def _(i):
        count = count_at(i)
        slots = [jnp.clip(tiles_at(i, e) - base, 0, NEAR - 1) for e in range(ENTRIES)]
        used = [(e < count).astype(jnp.int32) for e in range(ENTRIES)]
        firsts = []
        for e in range(ENTRIES):
            times = jnp.int32(0)
            before = jnp.int32(0)
            for other in range(ENTRIES):
                same = (slots[other] == slots[e]).astype(jnp.int32) * used[other]
                times = times + same
                if other < e:
                    before = before + same
            first = (before == 0).astype(jnp.int32) * used[e]
            bias = (1 - first).astype(F32) * MASKED
            for many in range(2, ENTRIES + 1):
                bias = bias + (first * (times == many).astype(jnp.int32)).astype(F32) * math.log2(many)
            firsts.append(first)
            slot_of[first_row + i, e] = slots[e]
            bias_of[first_row + i, e] = bias
        for j in range(NEAR):
            entry = jnp.int32(ENTRIES)
            for e in range(ENTRIES):
                entry = entry - (ENTRIES - e) * firsts[e] * (slots[e] == j).astype(jnp.int32)
            entry_of[first_row + i, j] = entry


def score(e, table, first_tile, slot_of, bias_of, kw, q, scores, best):
    s = dot(kw[first_tile + slot_of[table, e]], q, 1, 1)
    scores[e] = s
    return jnp.maximum(best, jnp.max(s.reshape(TILE // 8, 8, TILE), axis=0) + bias_of[table, e] * (1 / TO_LOG2))


def query_side(table, first_tile, at, slot_of, bias_of, vw, kt, vt, g, scores, weights, d_scores, g_low, best, score_next):
    top = jnp.max(best, axis=0, keepdims=True) * TO_LOG2
    total = jnp.zeros((8, TILE), F32)
    out_t = jnp.zeros((HEAD_DIM, TILE), F32)
    best_next = no_best()
    for e in range(ENTRIES):
        offset = top - bias_of[table, e]
        best_next = score_next(e, best_next)
        for part in range(TILE // PIECE):
            rows = slice(part * PIECE, (part + 1) * PIECE)
            p = jnp.exp2(scores[e, rows, :] * TO_LOG2 - offset)
            total = total + jnp.sum(p.reshape(PIECE // 8, 8, TILE), axis=0)
            weights[at, e, rows, :] = p.astype(BF16)
        out_t = out_t + dot(vt[first_tile + slot_of[table, e]], weights[at, e], 1, 0)
    inverse = 1.0 / jnp.sum(total, axis=0, keepdims=True)
    out_t = out_t * inverse
    g_t = (g.astype(F32).T * inverse).astype(BF16)
    g_low[at] = g_t
    row_dots = jnp.sum(g_t.astype(F32) * out_t, axis=0, keepdims=True)
    dq_t = jnp.zeros((HEAD_DIM, TILE), F32)
    for e in range(ENTRIES):
        dp = dot(vw[first_tile + slot_of[table, e]], g_t, 1, 0)
        ds = (weights[at, e].astype(F32) * (dp - row_dots)).astype(BF16)
        d_scores[at, e] = ds
        dq_t = dq_t + dot(kt[first_tile + slot_of[table, e]], ds, 1, 0)
    return out_t.T.astype(BF16), (dq_t * SCALE).T.astype(BF16), best_next


def no_best():
    return jnp.full((8, TILE), -3e38, F32)


def key_side(parts, entry_of, q_of, weights, d_scores, g_low):
    dk = jnp.zeros((TILE, HEAD_DIM), F32)
    dv = jnp.zeros((TILE, HEAD_DIM), F32)
    for table, at, task, j in parts:
        for i in range(TILES_DEV):
            dk = dk + dot(d_scores[at + i, entry_of[table + i, j]], q_of(task, i), 1, 0)
    for table, at, task, j in parts:
        for i in range(TILES_DEV):
            dv = dv + dot(weights[at + i, entry_of[table + i, j]], g_low[at + i], 1, 1)
    return dk * SCALE, dv


def kernel(
    frames, key_tiles, key_count, q_in, k_in, v_in, g_in, o_out, dq_out, dk_out, dv_out,
    far_table, slot_of, bias_of, entry_of, table_to, table_from, held, near_a, near_b, to_a, from_a, to_b, from_b, leaving,
    kw, vw, kt, vt, scores_even, scores_odd, weights, d_scores, g_low, dk_own, dv_own,
    in_send, in_recv, near_a_send, near_a_recv, near_b_send, near_b_recv, to_a_send, from_a_recv, to_b_send, from_b_recv,
    out_send, out_extra, out_recv, table_sems,
):
    frame = lax.axis_index("frames")
    rank = lax.axis_index("heads")
    core = frame % 2
    half = (frame // 2) % 2
    plane = (frame // 4) * 4
    row, side = rank // 2, rank % 2
    pair = flipped(rank, half)
    whole_head = pair * 3 + 2 * half
    split_head = pair * 3 + 1

    def device(of_frame, of_rank):
        return {"frames": of_frame, "heads": of_rank}

    def partner(offset):
        return ((row + offset[0]) % 4) * 2 + (side + offset[1]) % 2

    def member(of_half):
        return plane + 2 * of_half + core

    twin = device(frame + 1 - 2 * core, rank)
    above = device((frame + frames - 3 + 6 * core) % frames, rank)
    neighbours = []
    for step in (frames - 1, 1):
        there = (frame + step) % frames
        neighbours.append(device(there, flipped(pair, (there // 2) % 2)))
    table_peer = device(member(1 - half), flipped(rank, 1))

    barrier = pltpu.get_barrier_semaphore()
    greeted = [device(frame, partner(offset)) for offset in OFFSETS]
    greeted += [device(member(1 - half), partner(offset)) for offset in OFFSETS + ((0, 0),)]
    greeted += neighbours + [above]
    for peer in greeted:
        pl.semaphore_signal(barrier, inc=1, device_id=peer, device_id_type=MESH)

    table = jnp.zeros((8, 128), jnp.int32)
    at_row = lax.broadcasted_iota(jnp.int32, (8, 128), 0)
    at_lane = lax.broadcasted_iota(jnp.int32, (8, 128), 1)
    for i in range(TILES_DEV):
        for e in range(ENTRIES):
            table = jnp.where((at_row == i) & (at_lane == e), key_tiles[i, e], table)
        table = jnp.where((at_row == i) & (at_lane == ENTRIES), key_count[i], table)
    table_to[...] = table

    pl.semaphore_wait(barrier, len(greeted))

    def columns(head):
        return pl.ds(pl.multiple_of(head * HEAD_DIM, HEAD_DIM), HEAD_DIM)

    def token_rows(of_rank):
        return pl.ds(pl.multiple_of(of_rank * 128, 128), 128)

    def send(src, dst, send_sem, recv_sem, to):
        pltpu.make_async_remote_copy(
            src_ref=src, dst_ref=dst, send_sem=send_sem, recv_sem=recv_sem, device_id=to, device_id_type=MESH
        ).start()

    def wait_bytes(ref, sem):
        pltpu.make_async_copy(ref, ref, sem).wait()

    tensors = (q_in, k_in, v_in, g_in)
    outputs = (o_out, dq_out, dk_out, dv_out)

    def enter_whole(t):
        here = held.at[t, half, token_rows(rank), :]
        for turn in range(2):
            of_half = (half + turn) % 2
            for offset in OFFSETS + ((0, 0),) * turn:
                to = partner(offset)
                head = flipped(to, of_half) * 3 + 2 * of_half
                send(tensors[t].at[:, columns(head)], here, in_send.at[t, turn], in_recv.at[t, half], device(member(of_half), to))
        pltpu.make_async_copy(tensors[t].at[:, columns(whole_head)], here, in_recv.at[t, half]).start()

    def enter_split(t):
        here = held.at[t, 2, token_rows(rank), :]
        for offset in OFFSETS:
            to = partner(offset)
            send(tensors[t].at[:, columns(flipped(to, half) * 3 + 1)], here, in_send.at[t, 2], in_recv.at[t, 2], device(frame, to))
        pltpu.make_async_copy(tensors[t].at[:, columns(split_head)], here, in_recv.at[t, 2]).start()

    def leave_whole(t, task):
        there = outputs[t].at[:, columns(whole_head)]
        turn = (task + half) % 2
        for offset in OFFSETS:
            to = partner(offset)
            send(leaving.at[t, task, token_rows(to), :], there, out_send.at[t, task], out_recv.at[t, turn], device(member(task), to))

        @pl.when(turn == 0)
        def _():
            pltpu.make_async_copy(leaving.at[t, task, token_rows(rank), :], there, out_recv.at[t, 0]).start()

        @pl.when(turn == 1)
        def _():
            send(leaving.at[t, task, token_rows(rank), :], there, out_extra.at[t], out_recv.at[t, 1], device(member(1 - half), rank))

    def leave_split(t):
        there = outputs[t].at[:, columns(split_head)]
        for offset in OFFSETS:
            to = partner(offset)
            send(leaving.at[t, 2, token_rows(to), :], there, out_send.at[t, 2], out_recv.at[t, 2], device(frame, to))
        pltpu.make_async_copy(leaving.at[t, 2, token_rows(rank), :], there, out_recv.at[t, 2]).start()

    def wait_in(t, task):
        wait_bytes(held.at[t, task], in_recv.at[t, task])

    send(table_to, table_from, table_sems.at[0], table_sems.at[1], table_peer)
    first, second = 1 - core, core
    for t in (1, 2, 0, 3):
        enter_split(t)
    for kv in range(2):
        wait_in(1 + kv, 2)
        for way in range(2):
            send(
                held.at[1 + kv, 2], near_b.at[1 - way, kv], near_b_send.at[way, kv], near_b_recv.at[1 - way, kv], neighbours[way]
            )
    enter_whole(1)
    enter_whole(2)

    @pl.when(half == first)
    def _():
        enter_whole(0)
        enter_whole(3)

    make_tables(
        half * TILES_DEV, (frame - 1) * TILES_DEV, lambda i, e: key_tiles[i, e], lambda i: key_count[i], slot_of, bias_of, entry_of
    )
    wait_bytes(table_from, table_sems.at[1])
    pltpu.make_async_copy(table_from, far_table, table_sems.at[2]).start()
    for i in range(2 * TILES_DEV):
        weights[i, ENTRIES] = jnp.zeros((TILE, TILE), BF16)
        d_scores[i, ENTRIES] = jnp.zeros((TILE, TILE), BF16)
    pltpu.make_async_copy(table_from, far_table, table_sems.at[2]).wait()
    make_tables(
        (1 - half) * TILES_DEV, (member(1 - half) - 1) * TILES_DEV,
        lambda i, e: far_table[i, e], lambda i: far_table[i, ENTRIES], slot_of, bias_of, entry_of,
    )

    def spread(tile, kv, block):
        (kw, vw)[kv][tile] = block
        (kt, vt)[kv][tile] = block.T

    def take_near(slot, sem):
        for kv in range(2):
            wait_bytes(near_a.at[slot, kv], near_a_recv.at[sem, kv])

        @pl.loop(0, TILES_DEV)
        def _(j):
            for kv in range(2):
                spread(2 * slot * TILES_DEV + j, kv, near_a[slot, kv, tile_rows(j), :])

    def queries(task, table, first_tile, at):
        def score_of(i, scores):
            def one(e, best):
                return score(e, table + i, first_tile, slot_of, bias_of, kw, held[0, task, tile_rows(i), :], scores, best)

            return one

        def tile(i, scores, best, score_next):
            rows = tile_rows(i)
            out, dq, best = query_side(
                table + i, first_tile, at + i, slot_of, bias_of, vw, kt, vt, held[3, task, rows, :],
                scores, weights, d_scores, g_low, best, score_next,
            )
            leaving[0, task, rows, :] = out
            leaving[1, task, rows, :] = dq
            return best

        def two(k, best):
            best = tile(2 * k, scores_even, best, score_of(2 * k + 1, scores_odd))
            return tile(2 * k + 1, scores_odd, best, score_of((2 * k + 2) % TILES_DEV, scores_even))

        best = no_best()
        for e in range(ENTRIES):
            best = score_of(0, scores_even)(e, best)
        lax.fori_loop(0, TILES_DEV // 2, two, best)

    def q_of(task, i):
        return held[0, task, i * TILE : (i + 1) * TILE, :]

    def keys(put, *parts):
        @pl.loop(0, TILES_DEV, unroll=2)
        def _(j):
            dk, dv = key_side(
                [(table, at, task, j + part * TILES_DEV) for table, at, task, part in parts],
                entry_of, q_of, weights, d_scores, g_low,
            )
            put(tile_rows(j), dk, dv)

    def to_near(slot):
        def put(rows, dk, dv):
            to_a[slot, 0, rows, :] = dk.astype(BF16)
            to_a[slot, 1, rows, :] = dv.astype(BF16)

        return put

    def to_own(task):
        def put(rows, dk, dv):
            dk_own[task, rows, :] = dk
            dv_own[task, rows, :] = dv

        return put

    def whole_parts(task, part):
        return (task * TILES_DEV, task * TILES_DEV, task, part)

    def hand_over(slot, sem, at, to):
        for kv in range(2):
            send(to_a.at[slot, kv], from_a.at[at, kv], to_a_send.at[sem, kv], from_a_recv.at[at, kv], to)

    @pl.loop(0, TILES_DEV)
    def _(j):
        for kv in range(2):
            spread(WIDE + TILES_DEV + j, kv, held[1 + kv, 2, tile_rows(j), :])

    wait_in(0, 2)
    wait_in(3, 2)
    for way in range(2):
        for kv in range(2):
            wait_bytes(near_b.at[way, kv], near_b_recv.at[way, kv])

    @pl.loop(0, TILES_DEV)
    def _(j):
        for kv in range(2):
            for way in range(2):
                spread(WIDE + 2 * way * TILES_DEV + j, kv, near_b[way, kv, tile_rows(j), :])

    queries(2, half * TILES_DEV, WIDE, 0)

    for kv in range(2):
        for task in range(2):
            wait_in(1 + kv, task)
            send(
                held.at[1 + kv, task], near_a.at[task + core, kv], near_a_send.at[task, kv], near_a_recv.at[task, kv], twin
            )
        send(held.at[1 + kv, core], near_a.at[2 - 2 * core, kv], near_a_send.at[2, kv], near_a_recv.at[2, kv], above)

    @pl.when(half == second)
    def _():
        enter_whole(0)
        enter_whole(3)

    for way in (0, 1):
        def put(rows, dk, dv):
            to_b[way, 0, rows, :] = dk.astype(BF16)
            to_b[way, 1, rows, :] = dv.astype(BF16)

        keys(put, (half * TILES_DEV, 0, 2, 2 * way))
        for kv in range(2):
            send(to_b.at[way, kv], from_b.at[1 - way, kv], to_b_send.at[way, kv], from_b_recv.at[1 - way, kv], neighbours[way])
    leave_split(0)
    leave_split(1)
    keys(to_own(2), (half * TILES_DEV, 0, 2, 1))

    @pl.loop(0, TILES_DEV)
    def _(j):
        for kv in range(2):
            for task in range(2):
                spread((2 * task + 1) * TILES_DEV + j, kv, held[1 + kv, task, tile_rows(j), :])

    for task in range(2):
        take_near(task + 1 - core, task)

    wait_in(0, first)
    wait_in(3, first)
    queries(first, first * TILES_DEV, 2 * first * TILES_DEV, first * TILES_DEV)
    leave_whole(0, first)
    leave_whole(1, first)
    keys(to_near(2 * first), whole_parts(first, 2 * first))
    hand_over(2 * first, 0, first, twin)
    keys(to_own(first), whole_parts(first, 1))

    for way in range(2):
        for kv in range(2):
            wait_bytes(from_b.at[way, kv], from_b_recv.at[way, kv])

    @pl.loop(0, TILES_DEV)
    def _(j):
        rows = tile_rows(j)
        for kv, own in ((0, dk_own), (1, dv_own)):
            total = own[2, rows, :] + from_b[0, kv, rows, :].astype(F32) + from_b[1, kv, rows, :].astype(F32)
            leaving[2 + kv, 2, rows, :] = total.astype(BF16)

    leave_split(2)
    leave_split(3)

    take_near(2 * core, 2)
    wait_in(0, second)
    wait_in(3, second)
    queries(second, second * TILES_DEV, 2 * second * TILES_DEV, second * TILES_DEV)
    keys(to_near(2 * second), whole_parts(second, 2 * second))
    hand_over(2 * second, 1, 2, above)
    leave_whole(0, second)
    leave_whole(1, second)
    keys(to_near(1), whole_parts(0, 2), whole_parts(1, 0))
    hand_over(1, 2, second, twin)
    keys(to_own(second), whole_parts(second, 1))

    for task, others in ((first, (first,)), (second, (second, 2))):
        for kv, own in ((0, dk_own), (1, dv_own)):
            for at in others:
                wait_bytes(from_a.at[at, kv], from_a_recv.at[at, kv])

            @pl.loop(0, TILES_DEV)
            def _(j):
                rows = tile_rows(j)
                total = own[task, rows, :]
                for at in others:
                    total = total + from_a[at, kv, rows, :].astype(F32)
                leaving[2 + kv, task, rows, :] = total.astype(BF16)

            leave_whole(2 + kv, task)

    seven = SLAB - 128
    for t in range(4):
        wait_bytes(held.at[t, 0, 0:seven, :], in_send.at[t, 0])
        wait_bytes(held.at[t, 0], in_send.at[t, 1])
        wait_bytes(held.at[t, 0, 0:seven, :], in_send.at[t, 2])
        wait_bytes(leaving.at[t, 0, 0:128, :], out_extra.at[t])
        for task in range(3):
            wait_bytes(leaving.at[t, task, 0:seven, :], out_send.at[t, task])
            wait_bytes(leaving.at[t, task], out_recv.at[t, task])
    for kv in range(2):
        for at in range(3):
            wait_bytes(near_a.at[at, kv], near_a_send.at[at, kv])
            wait_bytes(to_a.at[at, kv], to_a_send.at[at, kv])
        for way in range(2):
            wait_bytes(near_b.at[way, kv], near_b_send.at[way, kv])
            wait_bytes(to_b.at[way, kv], to_b_send.at[way, kv])
    wait_bytes(table_to, table_sems.at[0])


def copy_out(*refs):
    sources, results, pieces, sems = refs[:4], refs[4:8], refs[8], refs[9]
    inward = [pltpu.make_async_copy(sources[t], pieces.at[t], sems.at[0, t]) for t in range(4)]
    outward = [pltpu.make_async_copy(pieces.at[t], results[t], sems.at[1, t]) for t in range(4)]
    for copy in inward:
        copy.start()
    for t in range(4):
        inward[t].wait()
        outward[t].start()
    for copy in outward:
        copy.wait()


def on_device(queries, key_rows, value_rows, out_grad, key_tiles, key_count):
    frames = lax.axis_size("frames")
    tokens, features = queries.shape

    def body(*refs):
        kernel(frames, *refs)

    hbm = pl.BlockSpec(memory_space=pl.ANY)
    smem = pl.BlockSpec(memory_space=pltpu.SMEM)
    dma = pltpu.SemaphoreType.DMA
    block = (SLAB, HEAD_DIM)
    shapes = [jax.ShapeDtypeStruct((tokens, features), BF16)] * 4
    results = pl.pallas_call(
        body,
        out_shape=shapes,
        in_specs=[smem, smem] + [hbm] * 4,
        out_specs=[hbm] * 4,
        scratch_shapes=[
            pltpu.SMEM((8, 128), jnp.int32),
            pltpu.SMEM((2 * TILES_DEV, ENTRIES), jnp.int32),
            pltpu.SMEM((2 * TILES_DEV, ENTRIES), F32),
            pltpu.SMEM((2 * TILES_DEV, NEAR), jnp.int32),
            pltpu.VMEM((8, 128), jnp.int32),
            pltpu.VMEM((8, 128), jnp.int32),
            pltpu.VMEM((4, 3) + block, BF16),
            pltpu.VMEM((3, 2) + block, BF16),
            pltpu.VMEM((2, 2) + block, BF16),
            pltpu.VMEM((3, 2) + block, BF16),
            pltpu.VMEM((3, 2) + block, BF16),
            pltpu.VMEM((2, 2) + block, BF16),
            pltpu.VMEM((2, 2) + block, BF16),
            pltpu.VMEM((4, 3) + block, BF16),
            pltpu.VMEM((WIDE + NEAR, TILE, HEAD_DIM), BF16),
            pltpu.VMEM((WIDE + NEAR, TILE, HEAD_DIM), BF16),
            pltpu.VMEM((WIDE + NEAR, HEAD_DIM, TILE), BF16),
            pltpu.VMEM((WIDE + NEAR, HEAD_DIM, TILE), BF16),
            pltpu.VMEM((ENTRIES, TILE, TILE), F32),
            pltpu.VMEM((ENTRIES, TILE, TILE), F32),
            pltpu.VMEM((2 * TILES_DEV, ENTRIES + 1, TILE, TILE), BF16),
            pltpu.VMEM((2 * TILES_DEV, ENTRIES + 1, TILE, TILE), BF16),
            pltpu.VMEM((2 * TILES_DEV, HEAD_DIM, TILE), BF16),
            pltpu.VMEM((3,) + block, F32),
            pltpu.VMEM((3,) + block, F32),
            dma((4, 3)),
            dma((4, 3)),
            dma((3, 2)),
            dma((3, 2)),
            dma((2, 2)),
            dma((2, 2)),
            dma((3, 2)),
            dma((3, 2)),
            dma((2, 2)),
            dma((2, 2)),
            dma((4, 3)),
            dma((4,)),
            dma((4, 3)),
            dma((3,)),
        ],
        compiler_params=pltpu.CompilerParams(collective_id=0, has_side_effects=True, vmem_limit_bytes=60 * 1024 * 1024),
        name="tile_attention",
    )(key_tiles, key_count, queries, key_rows, value_rows, out_grad)
    return pl.pallas_call(
        copy_out,
        out_shape=shapes,
        in_specs=[hbm] * 4,
        out_specs=[hbm] * 4,
        scratch_shapes=[pltpu.VMEM((4, tokens, features), BF16), dma((2, 4))],
        name="copy_out",
    )(*results)


def solution(mesh):
    spread = P(("frames", "heads"), None)
    return jax.shard_map(
        on_device,
        mesh=mesh,
        in_specs=(spread, spread, spread, spread, P("frames", None), P("frames")),
        out_specs=(spread, spread, spread, spread),
        check_vma=False,
    )
```

```python
import math

import jax
import jax.numpy as jnp
from jax import lax
from jax.experimental import pallas as pl
from jax.experimental.pallas import tpu as pltpu
from jax.sharding import PartitionSpec as P

HEAD_DIM = 128
TILE = 256
TILES_DEV = 4
ENTRIES = 8
NEAR = 3 * TILES_DEV
WIDE = 5 * TILES_DEV
SLAB = TILES_DEV * TILE
SCALE = HEAD_DIM**-0.5
TO_LOG2 = SCALE * math.log2(math.e)
MASKED = -1e30
PIECE = 32
F32 = jnp.float32
BF16 = jnp.bfloat16
MESH = pl.DeviceIdType.MESH
OFFSETS = ((0, 1), (1, 0), (3, 0), (2, 0), (1, 1), (3, 1), (2, 1))


def dot(a, b, a_dim, b_dim):
    return lax.dot_general(a, b, (((a_dim,), (b_dim,)), ((), ())), preferred_element_type=F32)


def tile_rows(tile):
    return pl.ds(pl.multiple_of(tile * TILE, TILE), TILE)


def flipped(index, flip):
    return index + flip * (1 - 2 * (index % 2))


def make_tables(first_row, base, tiles_at, count_at, slot_of, bias_of, entry_of):
    @pl.loop(0, TILES_DEV)
    def _(i):
        count = count_at(i)
        slots = [jnp.clip(tiles_at(i, e) - base, 0, NEAR - 1) for e in range(ENTRIES)]
        used = [(e < count).astype(jnp.int32) for e in range(ENTRIES)]
        firsts = []
        for e in range(ENTRIES):
            times = jnp.int32(0)
            before = jnp.int32(0)
            for other in range(ENTRIES):
                same = (slots[other] == slots[e]).astype(jnp.int32) * used[other]
                times = times + same
                if other < e:
                    before = before + same
            first = (before == 0).astype(jnp.int32) * used[e]
            bias = (1 - first).astype(F32) * MASKED
            for many in range(2, ENTRIES + 1):
                bias = bias + (first * (times == many).astype(jnp.int32)).astype(F32) * math.log2(many)
            firsts.append(first)
            slot_of[first_row + i, e] = slots[e]
            bias_of[first_row + i, e] = bias
        for j in range(NEAR):
            entry = jnp.int32(ENTRIES)
            for e in range(ENTRIES):
                entry = entry - (ENTRIES - e) * firsts[e] * (slots[e] == j).astype(jnp.int32)
            entry_of[first_row + i, j] = entry


def score(e, table, first_tile, slot_of, bias_of, kw, q, scores, best):
    s = dot(kw[first_tile + slot_of[table, e]], q, 1, 1)
    scores[e] = s
    return jnp.maximum(best, jnp.max(s.reshape(TILE // 8, 8, TILE), axis=0) + bias_of[table, e] * (1 / TO_LOG2))


def query_side(table, first_tile, at, slot_of, bias_of, vw, kt, vt, g, scores, weights, d_scores, g_low, best, score_next):
    top = jnp.max(best, axis=0, keepdims=True) * TO_LOG2
    total = jnp.zeros((8, TILE), F32)
    out_t = jnp.zeros((HEAD_DIM, TILE), F32)
    best_next = no_best()
    for e in range(ENTRIES):
        offset = top - bias_of[table, e]
        best_next = score_next(e, best_next)
        for part in range(TILE // PIECE):
            rows = slice(part * PIECE, (part + 1) * PIECE)
            p = jnp.exp2(scores[e, rows, :] * TO_LOG2 - offset)
            total = total + jnp.sum(p.reshape(PIECE // 8, 8, TILE), axis=0)
            weights[at, e, rows, :] = p.astype(BF16)
        out_t = out_t + dot(vt[first_tile + slot_of[table, e]], weights[at, e], 1, 0)
    inverse = 1.0 / jnp.sum(total, axis=0, keepdims=True)
    out_t = out_t * inverse
    g_t = (g.astype(F32).T * inverse).astype(BF16)
    g_low[at] = g_t
    row_dots = jnp.sum(g_t.astype(F32) * out_t, axis=0, keepdims=True)
    dq_t = jnp.zeros((HEAD_DIM, TILE), F32)
    for e in range(ENTRIES):
        dp = dot(vw[first_tile + slot_of[table, e]], g_t, 1, 0)
        ds = (weights[at, e].astype(F32) * (dp - row_dots)).astype(BF16)
        d_scores[at, e] = ds
        dq_t = dq_t + dot(kt[first_tile + slot_of[table, e]], ds, 1, 0)
    return out_t.T.astype(BF16), (dq_t * SCALE).T.astype(BF16), best_next


def no_best():
    return jnp.full((8, TILE), -3e38, F32)


def key_side(parts, entry_of, q_of, weights, d_scores, g_low):
    dk = jnp.zeros((TILE, HEAD_DIM), F32)
    dv = jnp.zeros((TILE, HEAD_DIM), F32)
    for table, at, task, j in parts:
        for i in range(TILES_DEV):
            dk = dk + dot(d_scores[at + i, entry_of[table + i, j]], q_of(task, i), 1, 0)
    for table, at, task, j in parts:
        for i in range(TILES_DEV):
            dv = dv + dot(weights[at + i, entry_of[table + i, j]], g_low[at + i], 1, 1)
    return dk * SCALE, dv


def kernel(
    frames, key_tiles, key_count, q_in, k_in, v_in, g_in, o_out, dq_out, dk_out, dv_out,
    far_table, slot_of, bias_of, entry_of, table_to, table_from, held, near_a, near_b, to_a, from_a, to_b, from_b, leaving,
    kw, vw, kt, vt, scores_even, scores_odd, weights, d_scores, g_low, dk_own, dv_own,
    in_send, in_recv, near_a_send, near_a_recv, near_b_send, near_b_recv, to_a_send, from_a_recv, to_b_send, from_b_recv,
    out_send, out_extra, out_recv, table_sems,
):
    frame = lax.axis_index("frames")
    rank = lax.axis_index("heads")
    core = frame % 2
    half = (frame // 2) % 2
    plane = (frame // 4) * 4
    row, side = rank // 2, rank % 2
    pair = flipped(rank, half)
    whole_head = pair * 3 + 2 * half
    split_head = pair * 3 + 1

    def device(of_frame, of_rank):
        return {"frames": of_frame, "heads": of_rank}

    def partner(offset):
        return ((row + offset[0]) % 4) * 2 + (side + offset[1]) % 2

    def member(of_half):
        return plane + 2 * of_half + core

    twin = device(frame + 1 - 2 * core, rank)
    above = device((frame + frames - 3 + 6 * core) % frames, rank)
    neighbours = []
    for step in (frames - 1, 1):
        there = (frame + step) % frames
        neighbours.append(device(there, flipped(pair, (there // 2) % 2)))
    table_peer = device(member(1 - half), flipped(rank, 1))

    barrier = pltpu.get_barrier_semaphore()
    greeted = [device(frame, partner(offset)) for offset in OFFSETS]
    greeted += [device(member(1 - half), partner(offset)) for offset in OFFSETS + ((0, 0),)]
    greeted += neighbours + [above]
    for peer in greeted:
        pl.semaphore_signal(barrier, inc=1, device_id=peer, device_id_type=MESH)

    table = jnp.zeros((8, 128), jnp.int32)
    at_row = lax.broadcasted_iota(jnp.int32, (8, 128), 0)
    at_lane = lax.broadcasted_iota(jnp.int32, (8, 128), 1)
    for i in range(TILES_DEV):
        for e in range(ENTRIES):
            table = jnp.where((at_row == i) & (at_lane == e), key_tiles[i, e], table)
        table = jnp.where((at_row == i) & (at_lane == ENTRIES), key_count[i], table)
    table_to[...] = table

    pl.semaphore_wait(barrier, len(greeted))

    def columns(head):
        return pl.ds(pl.multiple_of(head * HEAD_DIM, HEAD_DIM), HEAD_DIM)

    def token_rows(of_rank):
        return pl.ds(pl.multiple_of(of_rank * 128, 128), 128)

    def send(src, dst, send_sem, recv_sem, to):
        pltpu.make_async_remote_copy(
            src_ref=src, dst_ref=dst, send_sem=send_sem, recv_sem=recv_sem, device_id=to, device_id_type=MESH
        ).start()

    def wait_bytes(ref, sem):
        pltpu.make_async_copy(ref, ref, sem).wait()

    tensors = (q_in, k_in, v_in, g_in)
    outputs = (o_out, dq_out, dk_out, dv_out)

    def enter_whole(t):
        here = held.at[t, half, token_rows(rank), :]
        for turn in range(2):
            of_half = (half + turn) % 2
            for offset in OFFSETS + ((0, 0),) * turn:
                to = partner(offset)
                head = flipped(to, of_half) * 3 + 2 * of_half
                send(tensors[t].at[:, columns(head)], here, in_send.at[t, turn], in_recv.at[t, half], device(member(of_half), to))
        pltpu.make_async_copy(tensors[t].at[:, columns(whole_head)], here, in_recv.at[t, half]).start()

    def enter_split(t):
        here = held.at[t, 2, token_rows(rank), :]
        for offset in OFFSETS:
            to = partner(offset)
            send(tensors[t].at[:, columns(flipped(to, half) * 3 + 1)], here, in_send.at[t, 2], in_recv.at[t, 2], device(frame, to))
        pltpu.make_async_copy(tensors[t].at[:, columns(split_head)], here, in_recv.at[t, 2]).start()

    def leave_whole(t, task):
        there = outputs[t].at[:, columns(whole_head)]
        turn = (task + half) % 2
        for offset in OFFSETS:
            to = partner(offset)
            send(leaving.at[t, task, token_rows(to), :], there, out_send.at[t, task], out_recv.at[t, turn], device(member(task), to))

        @pl.when(turn == 0)
        def _():
            pltpu.make_async_copy(leaving.at[t, task, token_rows(rank), :], there, out_recv.at[t, 0]).start()

        @pl.when(turn == 1)
        def _():
            send(leaving.at[t, task, token_rows(rank), :], there, out_extra.at[t], out_recv.at[t, 1], device(member(1 - half), rank))

    def leave_split(t):
        there = outputs[t].at[:, columns(split_head)]
        for offset in OFFSETS:
            to = partner(offset)
            send(leaving.at[t, 2, token_rows(to), :], there, out_send.at[t, 2], out_recv.at[t, 2], device(frame, to))
        pltpu.make_async_copy(leaving.at[t, 2, token_rows(rank), :], there, out_recv.at[t, 2]).start()

    def wait_in(t, task):
        wait_bytes(held.at[t, task], in_recv.at[t, task])

    send(table_to, table_from, table_sems.at[0], table_sems.at[1], table_peer)
    first, second = 1 - core, core
    enter_whole(1)
    enter_whole(2)

    @pl.when(half == first)
    def _():
        enter_whole(0)
        enter_whole(3)

    enter_split(1)
    enter_split(2)

    @pl.when(half == second)
    def _():
        enter_whole(0)
        enter_whole(3)


    make_tables(
        half * TILES_DEV, (frame - 1) * TILES_DEV, lambda i, e: key_tiles[i, e], lambda i: key_count[i], slot_of, bias_of, entry_of
    )
    wait_bytes(table_from, table_sems.at[1])
    pltpu.make_async_copy(table_from, far_table, table_sems.at[2]).start()
    for i in range(2 * TILES_DEV):
        weights[i, ENTRIES] = jnp.zeros((TILE, TILE), BF16)
        d_scores[i, ENTRIES] = jnp.zeros((TILE, TILE), BF16)
    pltpu.make_async_copy(table_from, far_table, table_sems.at[2]).wait()
    make_tables(
        (1 - half) * TILES_DEV, (member(1 - half) - 1) * TILES_DEV,
        lambda i, e: far_table[i, e], lambda i: far_table[i, ENTRIES], slot_of, bias_of, entry_of,
    )

    for kv in range(2):
        for task in range(2):
            wait_in(1 + kv, task)
            send(
                held.at[1 + kv, task], near_a.at[task + core, kv], near_a_send.at[task, kv], near_a_recv.at[task, kv], twin
            )
        send(held.at[1 + kv, core], near_a.at[2 - 2 * core, kv], near_a_send.at[2, kv], near_a_recv.at[2, kv], above)

    def spread(tile, kv, block):
        (kw, vw)[kv][tile] = block
        (kt, vt)[kv][tile] = block.T

    @pl.loop(0, TILES_DEV)
    def _(j):
        for kv in range(2):
            for task in range(2):
                spread((2 * task + 1) * TILES_DEV + j, kv, held[1 + kv, task, tile_rows(j), :])

    def take_near(slot, sem):
        for kv in range(2):
            wait_bytes(near_a.at[slot, kv], near_a_recv.at[sem, kv])

        @pl.loop(0, TILES_DEV)
        def _(j):
            for kv in range(2):
                spread(2 * slot * TILES_DEV + j, kv, near_a[slot, kv, tile_rows(j), :])

    for task in range(2):
        take_near(task + 1 - core, task)

    def queries(task, table, first_tile, at, between=None):
        def score_of(i, scores):
            def one(e, best):
                return score(e, table + i, first_tile, slot_of, bias_of, kw, held[0, task, tile_rows(i), :], scores, best)

            return one

        def tile(i, scores, best, score_next):
            rows = tile_rows(i)
            out, dq, best = query_side(
                table + i, first_tile, at + i, slot_of, bias_of, vw, kt, vt, held[3, task, rows, :],
                scores, weights, d_scores, g_low, best, score_next,
            )
            leaving[0, task, rows, :] = out
            leaving[1, task, rows, :] = dq
            return best

        def two(k, best):
            best = tile(2 * k, scores_even, best, score_of(2 * k + 1, scores_odd))
            return tile(2 * k + 1, scores_odd, best, score_of((2 * k + 2) % TILES_DEV, scores_even))

        best = no_best()
        for e in range(ENTRIES):
            best = score_of(0, scores_even)(e, best)
        if between is None:
            lax.fori_loop(0, TILES_DEV // 2, two, best)
        else:
            best = two(0, best)
            between()
            two(1, best)

    def q_of(task, i):
        return held[0, task, i * TILE : (i + 1) * TILE, :]

    def keys(put, *parts):
        @pl.loop(0, TILES_DEV, unroll=2)
        def _(j):
            dk, dv = key_side(
                [(table, at, task, j + part * TILES_DEV) for table, at, task, part in parts],
                entry_of, q_of, weights, d_scores, g_low,
            )
            put(tile_rows(j), dk, dv)

    def to_near(slot):
        def put(rows, dk, dv):
            to_a[slot, 0, rows, :] = dk.astype(BF16)
            to_a[slot, 1, rows, :] = dv.astype(BF16)

        return put

    def to_own(task):
        def put(rows, dk, dv):
            dk_own[task, rows, :] = dk
            dv_own[task, rows, :] = dv

        return put

    def whole_parts(task, part):
        return (task * TILES_DEV, task * TILES_DEV, task, part)

    def hand_over(slot, sem, at, to):
        for kv in range(2):
            send(to_a.at[slot, kv], from_a.at[at, kv], to_a_send.at[sem, kv], from_a_recv.at[at, kv], to)

    wait_in(0, first)
    wait_in(3, first)
    queries(first, first * TILES_DEV, 2 * first * TILES_DEV, first * TILES_DEV)
    for kv in range(2):
        wait_in(1 + kv, 2)
        for way in range(2):
            send(
                held.at[1 + kv, 2], near_b.at[1 - way, kv], near_b_send.at[way, kv], near_b_recv.at[1 - way, kv], neighbours[way]
            )

    enter_split(0)
    enter_split(3)
    leave_whole(0, first)
    leave_whole(1, first)
    keys(to_near(2 * first), whole_parts(first, 2 * first))
    hand_over(2 * first, 0, first, twin)
    keys(to_own(first), whole_parts(first, 1))

    take_near(2 * core, 2)
    wait_in(0, second)
    wait_in(3, second)
    queries(second, second * TILES_DEV, 2 * second * TILES_DEV, second * TILES_DEV)
    leave_whole(0, second)
    leave_whole(1, second)
    keys(to_near(2 * second), whole_parts(second, 2 * second))
    hand_over(2 * second, 1, 2, above)
    keys(to_near(1), whole_parts(0, 2), whole_parts(1, 0))
    hand_over(1, 2, second, twin)
    keys(to_own(second), whole_parts(second, 1))

    wait_in(0, 2)
    wait_in(3, 2)
    for way in range(2):
        for kv in range(2):
            wait_bytes(near_b.at[way, kv], near_b_recv.at[way, kv])

    @pl.loop(0, TILES_DEV)
    def _(j):
        for kv in range(2):
            spread(j, kv, near_b[0, kv, tile_rows(j), :])
            spread(TILES_DEV + j, kv, held[1 + kv, 2, tile_rows(j), :])
            spread(2 * TILES_DEV + j, kv, near_b[1, kv, tile_rows(j), :])

    def finish_whole():
        for at in range(3):
            for kv in range(2):
                wait_bytes(from_a.at[at, kv], from_a_recv.at[at, kv])

        for task in range(2):
            border = (core == task).astype(F32)

            @pl.loop(0, TILES_DEV)
            def _(j):
                rows = tile_rows(j)
                for kv, own in ((0, dk_own), (1, dv_own)):
                    total = own[task, rows, :] + from_a[task, kv, rows, :].astype(F32)
                    total = total + border * from_a[2, kv, rows, :].astype(F32)
                    leaving[2 + kv, task, rows, :] = total.astype(BF16)

            leave_whole(2, task)
            leave_whole(3, task)

    queries(2, half * TILES_DEV, 0, 0, finish_whole)
    for way in (0, 1):
        def put(rows, dk, dv):
            to_b[way, 0, rows, :] = dk.astype(BF16)
            to_b[way, 1, rows, :] = dv.astype(BF16)

        keys(put, (half * TILES_DEV, 0, 2, 2 * way))
        for kv in range(2):
            send(to_b.at[way, kv], from_b.at[1 - way, kv], to_b_send.at[way, kv], from_b_recv.at[1 - way, kv], neighbours[way])
    leave_split(0)
    leave_split(1)

    keys(to_own(0), (half * TILES_DEV, 0, 2, 1))

    for kv, own in ((0, dk_own), (1, dv_own)):
        for way in range(2):
            wait_bytes(from_b.at[way, kv], from_b_recv.at[way, kv])

        @pl.loop(0, TILES_DEV)
        def _(j):
            rows = tile_rows(j)
            total = own[0, rows, :] + from_b[0, kv, rows, :].astype(F32) + from_b[1, kv, rows, :].astype(F32)
            leaving[2 + kv, 2, rows, :] = total.astype(BF16)

        leave_split(2 + kv)

    seven = SLAB - 128
    for t in range(4):
        wait_bytes(held.at[t, 0, 0:seven, :], in_send.at[t, 0])
        wait_bytes(held.at[t, 0], in_send.at[t, 1])
        wait_bytes(held.at[t, 0, 0:seven, :], in_send.at[t, 2])
        wait_bytes(leaving.at[t, 0, 0:128, :], out_extra.at[t])
        for task in range(3):
            wait_bytes(leaving.at[t, task, 0:seven, :], out_send.at[t, task])
            wait_bytes(leaving.at[t, task], out_recv.at[t, task])
    for kv in range(2):
        for at in range(3):
            wait_bytes(near_a.at[at, kv], near_a_send.at[at, kv])
            wait_bytes(to_a.at[at, kv], to_a_send.at[at, kv])
        for way in range(2):
            wait_bytes(near_b.at[way, kv], near_b_send.at[way, kv])
            wait_bytes(to_b.at[way, kv], to_b_send.at[way, kv])
    wait_bytes(table_to, table_sems.at[0])


def copy_out(*refs):
    sources, results, pieces, sems = refs[:4], refs[4:8], refs[8], refs[9]
    inward = [pltpu.make_async_copy(sources[t], pieces.at[t], sems.at[0, t]) for t in range(4)]
    outward = [pltpu.make_async_copy(pieces.at[t], results[t], sems.at[1, t]) for t in range(4)]
    for copy in inward:
        copy.start()
    for t in range(4):
        inward[t].wait()
        outward[t].start()
    for copy in outward:
        copy.wait()


def on_device(queries, key_rows, value_rows, out_grad, key_tiles, key_count):
    frames = lax.axis_size("frames")
    tokens, features = queries.shape

    def body(*refs):
        kernel(frames, *refs)

    hbm = pl.BlockSpec(memory_space=pl.ANY)
    smem = pl.BlockSpec(memory_space=pltpu.SMEM)
    dma = pltpu.SemaphoreType.DMA
    block = (SLAB, HEAD_DIM)
    shapes = [jax.ShapeDtypeStruct((tokens, features), BF16)] * 4
    results = pl.pallas_call(
        body,
        out_shape=shapes,
        in_specs=[smem, smem] + [hbm] * 4,
        out_specs=[hbm] * 4,
        scratch_shapes=[
            pltpu.SMEM((8, 128), jnp.int32),
            pltpu.SMEM((2 * TILES_DEV, ENTRIES), jnp.int32),
            pltpu.SMEM((2 * TILES_DEV, ENTRIES), F32),
            pltpu.SMEM((2 * TILES_DEV, NEAR), jnp.int32),
            pltpu.VMEM((8, 128), jnp.int32),
            pltpu.VMEM((8, 128), jnp.int32),
            pltpu.VMEM((4, 3) + block, BF16),
            pltpu.VMEM((3, 2) + block, BF16),
            pltpu.VMEM((2, 2) + block, BF16),
            pltpu.VMEM((3, 2) + block, BF16),
            pltpu.VMEM((3, 2) + block, BF16),
            pltpu.VMEM((2, 2) + block, BF16),
            pltpu.VMEM((2, 2) + block, BF16),
            pltpu.VMEM((4, 3) + block, BF16),
            pltpu.VMEM((WIDE, TILE, HEAD_DIM), BF16),
            pltpu.VMEM((WIDE, TILE, HEAD_DIM), BF16),
            pltpu.VMEM((WIDE, HEAD_DIM, TILE), BF16),
            pltpu.VMEM((WIDE, HEAD_DIM, TILE), BF16),
            pltpu.VMEM((ENTRIES, TILE, TILE), F32),
            pltpu.VMEM((ENTRIES, TILE, TILE), F32),
            pltpu.VMEM((2 * TILES_DEV, ENTRIES + 1, TILE, TILE), BF16),
            pltpu.VMEM((2 * TILES_DEV, ENTRIES + 1, TILE, TILE), BF16),
            pltpu.VMEM((2 * TILES_DEV, HEAD_DIM, TILE), BF16),
            pltpu.VMEM((2,) + block, F32),
            pltpu.VMEM((2,) + block, F32),
            dma((4, 3)),
            dma((4, 3)),
            dma((3, 2)),
            dma((3, 2)),
            dma((2, 2)),
            dma((2, 2)),
            dma((3, 2)),
            dma((3, 2)),
            dma((2, 2)),
            dma((2, 2)),
            dma((4, 3)),
            dma((4,)),
            dma((4, 3)),
            dma((3,)),
        ],
        compiler_params=pltpu.CompilerParams(collective_id=0, has_side_effects=True, vmem_limit_bytes=60 * 1024 * 1024),
        name="tile_attention",
    )(key_tiles, key_count, queries, key_rows, value_rows, out_grad)
    return pl.pallas_call(
        copy_out,
        out_shape=shapes,
        in_specs=[hbm] * 4,
        out_specs=[hbm] * 4,
        scratch_shapes=[pltpu.VMEM((4, tokens, features), BF16), dma((2, 4))],
        name="copy_out",
    )(*results)


def solution(mesh):
    spread = P(("frames", "heads"), None)
    return jax.shard_map(
        on_device,
        mesh=mesh,
        in_specs=(spread, spread, spread, spread, P("frames", None), P("frames")),
        out_specs=(spread, spread, spread, spread),
        check_vma=False,
    )
```
